128 devices in a mesh: pole: 8 (over x_lo, z), row: 4 (over x_hi, core), col: 4 (over y).
Axes of the slice: x: 4 (x_hi: 2, x_lo: 2; x = x_hi * 2 + x_lo), y: 4, z: 4, core: 2. Of those that a mesh axis runs over, the one named last changes fastest.
Arguments:
- inverse_tile: float32 [8, 2, 4608, 4608], P('pole', None, 'row', 'col'), may hold values from -0.0625 to 0.0625
- lower_factor: float32 [8, 2, 256, 4608], P('pole', None, 'row', 'col'), may hold values from -6 to 6
- upper_factor: float32 [8, 2, 256, 4608], P('pole', None, 'col', 'row'), may hold values from -1.5 to 1.5
- pivot_inverse: float32 [8, 2, 256, 256], P('pole', None, 'row', 'col'), may hold values from -48 to 48
- pole_weights: float32 [8, 2], P('pole'), may hold values from -3 to 3
- block_owners: int32 [2304, 6], replicated, may hold values from 0 to 127, all different within a row; in each aligned block of 18 rows (0 to 17, 18 to 35, ...) at most 2 rows name the same one
- basis_ancestor: float32 [4608, 16384], P(None, ('pole', 'row', 'col')), may hold values from -3 to 3
- basis_super: float32 [256, 16384], P(None, ('pole', 'row', 'col')), may hold values from -0.09375 to 0.09375
Outputs:
- upper_density: float32 [256, 4608], P(('pole', 'row'), 'col')
- charge: float32 [16384], P(('pole', 'row', 'col'))
The draws below stay inside these ranges and needn't reach their ends.
Inputs may be any that keep to these rules, and one draw needn't show every extreme that they name: `block_owners`: each row names 6 different owners. Among the rows k * 18 to (k + 1) * 18 - 1, for each k, no owner is named more than 2 times, and in every draw some owner is named exactly 2 times there. Every owner is named by some row.
All inputs are finite; a program needn't handle non-finite values.
Results may differ from the reference program's by a relative error of at most 0.0003.
Values sent between devices are 32-bit elements; how exact they have to be, the bound alone decides.
A program may use at most 64 MiB of HBM per device.

```python
import math
import jax
import jax.numpy as jnp
import numpy as np
from jax import lax

S = 256
R = 4608
POLES = 8
NB = 18
TOPK = 6
GP = 128
BR = 2
NBLK = 2304
CAP = 2
GRID = 16384
DEVICES = 128


def levels(own_key, shape, split, low, largest):
    loudness, own = 1.0, jax.random.fold_in(own_key, 6)
    for axis_at, blocks in split:
        draws = jnp.exp(jax.random.uniform(jax.random.fold_in(own, axis_at), (blocks,), jnp.float32, low / len(split), largest / len(split)))
        loudness = loudness * jnp.repeat(draws, shape[axis_at] // blocks).reshape([-1 if axis == axis_at else 1 for axis in range(len(shape))])
    return loudness


def assign_block(stream_key, own, number, rows, count, top, most, slope):
    ranking = jax.random.permutation(stream_key, count)
    crowded, usual = portions_of(count, rows * top, most, slope, True), portions_of(count, rows * top, most, slope, False)
    places = jnp.arange(count)

    def named(sizes, rotation):
        used = int((sizes > 0).sum())
        fixed = max(1, used // 4)
        moved = fixed + (places - fixed + rotation * (used - fixed)) % max(1, count - fixed)
        return jnp.zeros((count,), jnp.int32).at[ranking[jnp.where(places < fixed, places, moved)]].set(jnp.asarray(sizes, jnp.int32))

    sizes = jnp.where(number % 4 == 0, named(crowded, number // 4), named(usual, number - number // 4 - 1))
    mixed = jax.random.permutation(jax.random.fold_in(own, 3), count)
    source_of, taker = mixed[0:count // 2 * 2:2], mixed[1:count // 2 * 2:2]
    margin = jnp.minimum(sizes[source_of] - 1, most - sizes[taker]) // 2
    margin = jnp.where((source_of == ranking[0]) | (taker == ranking[0]) | (sizes[taker] == 0), 0, jnp.maximum(margin, 0))
    moved = jax.random.randint(jax.random.fold_in(own, 4), (count // 2,), 0, 1 << 20) % (margin + 1)
    sizes = sizes.at[source_of].add(-moved).at[taker].add(moved)
    items = jnp.searchsorted(jnp.cumsum(sizes), jnp.arange(rows * top), side="right").astype(jnp.int32)
    table = items.reshape(top, rows).T
    table = table[jax.random.permutation(jax.random.fold_in(own, 1), rows)]
    rotation = jax.random.randint(jax.random.fold_in(own, 2), (rows, 1), 0, top)
    return jnp.take_along_axis(table, (jnp.arange(top)[None, :] + rotation) % top, axis=1)


def portions_of(count, total, reach, skew, full):
    weights = [(1 << 20) // math.isqrt(standing ** skew) + 1 for standing in range(1, count + 1)]
    largest = reach if full else min(reach, max(-(-total // count), total * weights[0] // sum(weights)))
    least = 1 if total - largest >= count - 1 else 0
    holding, surplus = [largest] + [least] * (count - 1), total - largest - least * (count - 1)
    while surplus > 0:
        free = [i for i in range(1, count) if holding[i] < largest] or [i for i in range(1, count) if holding[i] < reach]
        mass, left = sum([weights[i] for i in free]), surplus
        for i in free:
            more = min(reach - holding[i], max(1, left * weights[i] // mass), surplus)
            holding[i] = holding[i] + more
            surplus = surplus - more
    return np.array(holding)


def noise(rng, shape, width, most, split=(), kind=jnp.bfloat16):
    entries = width * jax.random.normal(rng, shape, jnp.float32)
    if split:
        entries = entries * levels(rng, shape, split, -0.22, 0.18)
    return jnp.clip(entries, -most, most).astype(kind)


def setup_inputs(seed: int = 0) -> dict:
    seeds = jax.random.split(jax.random.key(seed), 9)
    inverse_tile = noise(seeds[0], (POLES, 2, R, R), (2 * R) ** -0.5, 0.0625, ((0, 8), (2, 4), (3, 4)), jnp.float32)
    lower_factor = noise(seeds[1], (POLES, 2, S, R), 1.0, 6.0, ((0, 8), (2, 4), (3, 4)), jnp.float32)
    upper_factor = noise(seeds[2], (POLES, 2, S, R), 0.25, 1.5, ((0, 8), (2, 4), (3, 4)), jnp.float32)
    pivot_inverse = noise(seeds[3], (POLES, 2, S, S), 8.0, 48.0, ((0, 8), (2, 4), (3, 4)), jnp.float32)
    pole_weights = noise(seeds[4], (POLES, 2), 0.5, 3.0, ((0, 8),), jnp.float32)
    block_owners_keys = jax.random.split(jax.random.fold_in(seeds[5], 1), NBLK // NB)
    block_owners_turns = jax.random.permutation(jax.random.fold_in(seeds[5], 3), NBLK // NB)
    block_owners = jax.vmap(lambda own, number: assign_block(jax.random.fold_in(seeds[5], 2), own, number, NB, DEVICES, TOPK, CAP, 2))(block_owners_keys, block_owners_turns).reshape((NBLK, TOPK))
    basis_ancestor = noise(seeds[6], (R, GRID), 0.5, 3.0, ((1, 128),), jnp.float32)
    basis_super = noise(seeds[7], (S, GRID), 4096 ** -0.5, 0.09375, ((1, 128),), jnp.float32)
    return dict(inverse_tile=inverse_tile, lower_factor=lower_factor, upper_factor=upper_factor, pivot_inverse=pivot_inverse, pole_weights=pole_weights, block_owners=block_owners, basis_ancestor=basis_ancestor, basis_super=basis_super)


def product(left, right):
    return jnp.dot(left, right, precision=lax.Precision.HIGHEST, preferred_element_type=jnp.float32)


def product_t(left, right):
    return lax.dot_general(left, right, (((1,), (1,)), ((), ())), precision=lax.Precision.HIGHEST, preferred_element_type=jnp.float32)


def reference(inverse_tile, lower_factor, upper_factor, pivot_inverse, pole_weights, block_owners, basis_ancestor, basis_super):
    def per_pole(carry, items):
        tile, lower_t, upper, pivot, weight = items
        lower_sum, upper_sum, pivot_sum = carry
        al_re = product_t(tile[0], lower_t[0]) - product_t(tile[1], lower_t[1])
        al_im = product_t(tile[0], lower_t[1]) + product_t(tile[1], lower_t[0])
        ua_re = product(upper[0], tile[0]) - product(upper[1], tile[1])
        ua_im = product(upper[0], tile[1]) + product(upper[1], tile[0])
        ual_re = product(upper[0], al_re) - product(upper[1], al_im)
        ual_im = product(upper[0], al_im) + product(upper[1], al_re)
        lower_sum = lower_sum - (weight[0] * al_im + weight[1] * al_re)
        upper_sum = upper_sum - (weight[0] * ua_im + weight[1] * ua_re)
        pivot_sum = pivot_sum + weight[0] * (pivot[1] + ual_im) + weight[1] * (pivot[0] + ual_re)
        return (lower_sum, upper_sum, pivot_sum), None

    start = (jnp.zeros((R, S), jnp.float32), jnp.zeros((S, R), jnp.float32), jnp.zeros((S, S), jnp.float32))
    (lower_density, upper_density, pivot_density), unused = lax.scan(
        per_pole, start, (inverse_tile, lower_factor, upper_factor, pivot_inverse, pole_weights))

    def per_owner(owner):
        routed = jnp.any(block_owners == owner, axis=1).astype(jnp.float32)
        row_mask = jnp.repeat(routed, BR)
        offset = (owner * GP).astype(jnp.int32)
        super_cols = lax.dynamic_slice_in_dim(basis_super, offset, GP, 1)
        ances_cols = lax.dynamic_slice_in_dim(basis_ancestor, offset, GP, 1)
        projected = product(lower_density, super_cols)
        ancestor_part = jnp.sum(row_mask[:, None] * ances_cols * projected, 0)
        pivot_part = jnp.sum(super_cols * product(pivot_density, super_cols), 0)
        return ancestor_part + pivot_part

    charge = lax.map(per_owner, jnp.arange(DEVICES, dtype=jnp.int32)).reshape(GRID)
    return upper_density, charge
```

```python
import jax
import jax.numpy as jnp
from jax import lax
from jax.experimental import pallas as pl
from jax.experimental.pallas import tpu as pltpu
from jax.sharding import PartitionSpec as P

MESH = pl.DeviceIdType.MESH
F32 = jnp.float32
BF16 = jnp.bfloat16
T = 1152
S = 256
Q = 64
NB = 18
TOPK = 6
DEV = 128
CHUNKS = ((0, 512), (512, 512), (1024, 128))
BLK = 288
SUB = 72
W = T + S


def nt(a, b):
    return lax.dot_general(a, b, (((1,), (1,)), ((), ())), preferred_element_type=F32)


def nn(a, b):
    return jnp.dot(a, b, preferred_element_type=F32)


def split(v):
    hi = v.astype(BF16)
    return hi, (v - hi.astype(F32)).astype(BF16)


def rows_of(start, size):
    return pl.ds(pl.multiple_of(start, 8), size)


def kernel(
    w_ref, a_hbm, l_hbm, u_hbm, piv_ref,
    upper_out, lower_out, pv_out,
    a32, ah, al, lf, uf, relay, bl, br, uph, upl, xr, xi, xih, xil, xrh, xrl, y, lt,
    rz1, rz2, ry1, ry2, rx, cb, rc, ru1, ru2, rv1, rv2, pb,
    sends, recvs, locs,
):
    pole, row, col = lax.axis_index("pole"), lax.axis_index("row"), lax.axis_index("col")
    x_lo, z = pole // 4, pole % 4
    x_hi, core = row // 2, row % 2
    x = x_hi * 2 + x_lo

    def at_x(v):
        return ((v % 2) * 4 + z, (v // 2) * 2 + core, col)

    def row_x(v):
        return (v // 2) * 2 + core

    xp, xm, x2 = (x + 1) % 4, (x + 3) % 4, (x + 2) % 4
    yp, ym, y2 = (col + 1) % 4, (col + 3) % 4, (col + 2) % 4
    zp, zm, z2 = (z + 1) % 4, (z + 3) % 4, (z + 2) % 4
    d_core = (pole, x_hi * 2 + 1 - core, col)
    d_xp, d_xm = at_x(xp), at_x(xm)
    d_yp, d_ym, d_y2 = (pole, row, yp), (pole, row, ym), (pole, row, y2)
    d_zp, d_zm = (x_lo * 4 + zp, row, col), (x_lo * 4 + zm, row, col)
    d_xn = at_x(x_hi * 2 + 1 - x_lo)
    started = []

    def send(src, dst, dev):
        n = len(started)
        c = pltpu.make_async_remote_copy(
            src_ref=src, dst_ref=dst, send_sem=sends.at[n], recv_sem=recvs.at[n],
            device_id=dev, device_id_type=MESH,
        )
        c.start()
        started.append(c)
        return c

    local_a = []
    for b in range(4):
        rs = slice(b * BLK, (b + 1) * BLK)
        c = pltpu.make_async_copy(a_hbm.at[0, :, rs, :], a32.at[:, rs, :], locs.at[b])
        local_a.append(c)
    local_l = pltpu.make_async_copy(l_hbm.at[0], lf.at[row], locs.at[4])
    local_u = pltpu.make_async_copy(u_hbm.at[0], uf.at[col], locs.at[5])
    local_l.start()
    local_a[0].start()
    local_a[1].start()

    barrier = pltpu.get_barrier_semaphore()
    for dev in (d_core, d_xp, d_xm, d_yp, d_ym, d_y2, d_zp, d_zm):
        pl.semaphore_signal(barrier, inc=1, device_id=dev, device_id_type=MESH)
    pl.semaphore_wait(barrier, 8)

    def lanes(k):
        return pl.ds(CHUNKS[k][0], CHUNKS[k][1])

    def l_own(k):
        return (
            send(l_hbm.at[0, 0, :, lanes(k)], relay.at[0, :, lanes(k)], d_xp),
            send(l_hbm.at[0, 1, :, lanes(k)], relay.at[1, :, lanes(k)], d_xm),
        )

    def l_relay(k, own):
        own[0].wait_recv()
        p = send(relay.at[0, :, lanes(k)], lf.at[row_x(xm), 0, :, lanes(k)], d_xp)
        own[1].wait_recv()
        m = send(relay.at[1, :, lanes(k)], lf.at[row_x(xp), 1, :, lanes(k)], d_xm)
        return p, m

    far = (1 - x_hi) * 2 + core

    def l_share(k, pair):
        pair[0].wait_recv()
        pair[1].wait_recv()
        return send(lf.at[far, :, :, lanes(k)], lf.at[far, :, :, lanes(k)], d_core)

    def u_own(k):
        return (
            send(u_hbm.at[0, :, :, lanes(k)], uf.at[col, :, :, lanes(k)], d_yp),
            send(u_hbm.at[0, :, :, lanes(k)], uf.at[col, :, :, lanes(k)], d_ym),
        )

    def u_forward(k, own):
        own[0].wait_recv()
        p = send(uf.at[ym, 0, :, lanes(k)], uf.at[ym, 0, :, lanes(k)], d_yp)
        own[1].wait_recv()
        m = send(uf.at[yp, 1, :, lanes(k)], uf.at[yp, 1, :, lanes(k)], d_ym)
        return p, m

    l_near = send(l_hbm.at[0], lf.at[row], d_core)
    lo = [l_own(0)]
    uo = [u_own(0)]
    lo.append(l_own(1))
    uo.append(u_own(1))
    local_a[2].start()
    local_a[3].start()
    local_u.start()

    w_re, w_im = w_ref[0, 0], w_ref[0, 1]

    def build(dst, slot, q, lane):
        re, im = lf[slot, 0, :, lane], lf[slot, 1, :, lane]
        a, b = pl.ds(q * Q, Q), pl.ds(2 * Q + q * Q, Q)
        rh, rl = split(re)
        ih, il = split(im)
        dst[0, a, lane], dst[1, a, lane] = rh, rl
        dst[0, b, lane], dst[1, b, lane] = ih, il
        dst[2, a, lane], dst[3, a, lane] = -ih, -il
        dst[2, b, lane], dst[3, b, lane] = rh, rl

    def product(rs, lane, b):
        acc = nt(ah[0, rs, lane], b[0, :, lane])
        acc = acc + nt(ah[0, rs, lane], b[1, :, lane])
        acc = acc + nt(al[0, rs, lane], b[0, :, lane])
        acc = acc + nt(ah[1, rs, lane], b[2, :, lane])
        acc = acc + nt(ah[1, rs, lane], b[3, :, lane])
        acc = acc + nt(al[1, rs, lane], b[2, :, lane])
        return acc

    def split_a(b):
        local_a[b].wait()

        @pl.loop(0, BLK // 16)
        def _(i):
            rs = pl.ds(pl.multiple_of(b * BLK + i * 16, 16), 16)
            for part in range(2):
                hi, low = split(a32[part, rs, :])
                ah[part, rs, :] = hi
                al[part, rs, :] = low

    whole = pl.ds(0, T)

    def near(b):
        rs = pl.ds(b * BLK, BLK)
        acc = product(rs, whole, bl)
        xr[x_hi, rs, :] = acc[:, :128]
        xi[x_hi, rs, :] = acc[:, 128:]

    local_l.wait()
    l_near.wait_recv()
    for q in range(2):
        build(bl, x_hi * 2 + q, q, whole)
    split_a(0)
    near(0)
    split_a(1)
    lr = [l_relay(0, lo[0])]
    lo.append(l_own(2))
    near(1)
    split_a(2)
    lr.append(l_relay(1, lo[1]))
    uf_moves = [u_forward(0, uo[0])]
    uo.append(u_own(2))
    near(2)
    ls = [l_share(0, lr[0])]
    lr.append(l_relay(2, lo[2]))
    split_a(3)
    near(3)

    def far_chunk(k):
        for q in range(2):
            build(br, (1 - x_hi) * 2 + q, q, lanes(k))

        @pl.loop(0, 4)
        def _(b):
            rs = pl.ds(pl.multiple_of(b * BLK, 16), BLK)
            acc = product(rs, lanes(k), br)
            if k == 0:
                xr[1 - x_hi, rs, :] = acc[:, :128]
                xi[1 - x_hi, rs, :] = acc[:, 128:]
            else:
                xr[1 - x_hi, rs, :] += acc[:, :128]
                xi[1 - x_hi, rs, :] += acc[:, 128:]

    ls[0].wait_recv()
    far_chunk(0)
    ls.append(l_share(1, lr[1]))
    uf_moves.append(u_forward(1, uo[1]))
    ls.append(l_share(2, lr[2]))
    ls[1].wait_recv()
    far_chunk(1)
    uf_moves.append(u_forward(2, uo[2]))
    ls[2].wait_recv()
    far_chunk(2)

    @pl.loop(0, 4)
    def _(b):
        rs = pl.ds(pl.multiple_of(b * BLK, 16), BLK)
        for h in range(2):
            lt[h, rs, :] = -(w_re * xi[h, rs, :] + w_im * xr[h, rs, :])

    def zblk(b):
        return rows_of(b * BLK, BLK)

    c1p = send(lt.at[0, zblk(z2), :], rz1.at[0], d_zp)
    c1m = send(lt.at[1, zblk(z2), :], rz1.at[1], d_zm)

    local_u.wait()

    def upper_chunk(k):
        lane = lanes(k)
        for q in range(4):
            re, im = uf[q, 0, :, lane], uf[q, 1, :, lane]
            rs = pl.ds(q * Q, Q)
            for part, v in ((0, w_re * re - w_im * im), (1, w_re * im + w_im * re)):
                hi, low = split(v)
                uph[part, rs, lane] = hi
                upl[part, rs, lane] = low
        acc = nn(uph[0, :, lane], ah[1, lane, :])
        acc = acc + nn(uph[0, :, lane], al[1, lane, :])
        acc = acc + nn(upl[0, :, lane], ah[1, lane, :])
        acc = acc + nn(uph[1, :, lane], ah[0, lane, :])
        acc = acc + nn(uph[1, :, lane], al[0, lane, :])
        acc = acc + nn(upl[1, :, lane], ah[0, lane, :])
        if k == 0:
            y[...] = acc
        else:
            y[...] += acc

    for h in range(2):
        hs = pl.ds(h * 128, 128)
        hi, low = split(xi[h])
        xih[:, hs], xil[:, hs] = hi, low
        hi, low = split(xr[h])
        xrh[:, hs], xrl[:, hs] = hi, low

    for c in uf_moves[0]:
        c.wait_recv()
    c1p.wait_recv()
    lt[0, zblk(zp), :] += rz1[0]
    c2p = send(lt.at[:, zblk(zp), :], rz2.at[0], d_zp)
    c1m.wait_recv()
    lt[1, zblk(zm), :] += rz1[1]
    c2m = send(lt.at[:, zblk(zm), :], rz2.at[1], d_zm)
    upper_chunk(0)
    for c in uf_moves[1]:
        c.wait_recv()
    upper_chunk(1)
    for c in uf_moves[2]:
        c.wait_recv()
    upper_chunk(2)

    def yblk(b):
        return rows_of(z * BLK + b * SUB, SUB)

    c2p.wait_recv()
    c2m.wait_recv()
    for h in range(2):
        lt[h, zblk(z), :] += rz2[0, h] + rz2[1, h]
    e1p = send(lt.at[0, yblk(y2), :], ry1.at[0], d_yp)
    e1m = send(lt.at[1, yblk(y2), :], ry1.at[1], d_ym)

    pv = nn(uph[0], xih[...])
    pv = pv + nn(uph[0], xil[...])
    pv = pv + nn(upl[0], xih[...])
    pv = pv + nn(uph[1], xrh[...])
    pv = pv + nn(uph[1], xrl[...])
    pv = pv + nn(upl[1], xrh[...])
    place = (
        lax.broadcasted_iota(jnp.int32, (Q, S), 1)
        == lax.broadcasted_iota(jnp.int32, (Q, S), 0) + col * Q
    ).astype(F32)
    piece = w_re * piv_ref[0, 1] + w_im * piv_ref[0, 0]
    placed = jnp.dot(piece, place, precision=lax.Precision.HIGHEST, preferred_element_type=F32)
    y_pv = y
    for g in range(32):
        rs = slice(g * 8, g * 8 + 8)
        at = (g % 2, (g // 4) % 4, ((g // 2) % 2) * 2 + g // 16)
        mine = (row == g // 8).astype(F32)
        cb[at[0], at[1], at[2], :, :T] = -y_pv[rs, :]
        cb[at[0], at[1], at[2], :, T:] = pv[rs, :] + mine * placed[(g % 8) * 8 : (g % 8) * 8 + 8, :]
    to_core = send(cb.at[1 - core], rc, d_core)

    e1p.wait_recv()
    lt[0, yblk(yp), :] += ry1[0]
    e2p = send(lt.at[:, yblk(yp), :], ry2.at[0], d_yp)
    e1m.wait_recv()
    lt[1, yblk(ym), :] += ry1[1]
    e2m = send(lt.at[:, yblk(ym), :], ry2.at[1], d_ym)

    to_core.wait_recv()

    @pl.loop(0, 4)
    def _(b):
        cb[core, b] += rc[b]

    f1p = send(cb.at[core, z2, pl.ds(0, 2)], ru1.at[0], d_zp)
    f1m = send(cb.at[core, z2, pl.ds(2, 2)], ru1.at[1], d_zm)

    e2p.wait_recv()
    e2m.wait_recv()
    for h in range(2):
        lt[h, yblk(col), :] += ry2[0, h] + ry2[1, h]
    g1 = send(lt.at[:, yblk(col), :], rx, d_xn)

    f1p.wait_recv()
    cb[core, zp, 0:2] += ru1[0]
    f2p = send(cb.at[core, zp], ru2.at[0], d_zp)
    f1m.wait_recv()
    cb[core, zm, 2:4] += ru1[1]
    f2m = send(cb.at[core, zm], ru2.at[1], d_zm)

    g1.wait_recv()
    for h in range(2):
        lower_out[:, h * 128 : (h + 1) * 128] = lt[h, yblk(col), :] + rx[h]

    f2p.wait_recv()
    f2m.wait_recv()
    cb[core, z] += ru2[0] + ru2[1]
    h1p = send(cb.at[core, z, x2, :, pl.ds(0, 768)], rv1.at[0, :, pl.ds(0, 768)], d_xp)
    h1m = send(cb.at[core, z, x2, :, pl.ds(768, 640)], rv1.at[1, :, pl.ds(0, 640)], d_xm)
    h1p.wait_recv()
    cb[core, z, xp, :, :768] += rv1[0]
    h2p = send(cb.at[core, z, xp], rv2.at[0], d_xp)
    h1m.wait_recv()
    cb[core, z, xm, :, 768:] += rv1[1, :, :640]
    h2m = send(cb.at[core, z, xm], rv2.at[1], d_xm)
    h2p.wait_recv()
    h2m.wait_recv()
    total = cb[core, z, x] + rv2[0] + rv2[1]
    upper_out[...] = total[:, :T]
    pb[col] = total[:, T:]
    last = [send(pb.at[col], pb.at[col], dev) for dev in (d_yp, d_ym, d_y2)]
    for c in last:
        c.wait_recv()
    pv_out[...] = pb[0] + pb[1] + pb[2] + pb[3]
    for c in started:
        c.wait_send()


N_COPIES = 1 + 6 + 6 + 6 + 6 + 3 + 4 + 4 + 1 + 1 + 4 + 4 + 3


def dense_part(weights, tile, lower, upper, pivot):
    vmem = pl.BlockSpec(memory_space=pltpu.VMEM)
    hbm = pl.BlockSpec(memory_space=pl.ANY)
    return pl.pallas_call(
        kernel,
        out_shape=(
            jax.ShapeDtypeStruct((8, T), F32),
            jax.ShapeDtypeStruct((SUB, S), F32),
            jax.ShapeDtypeStruct((8, S), F32),
        ),
        in_specs=[pl.BlockSpec(memory_space=pltpu.SMEM), hbm, hbm, hbm, vmem],
        out_specs=(vmem, vmem, vmem),
        scratch_shapes=[
            pltpu.VMEM((2, T, T), F32),
            pltpu.VMEM((2, T, T), BF16),
            pltpu.VMEM((2, T, T), BF16),
            pltpu.VMEM((4, 2, Q, T), F32),
            pltpu.VMEM((4, 2, Q, T), F32),
            pltpu.VMEM((2, Q, T), F32),
            pltpu.VMEM((4, S, T), BF16),
            pltpu.VMEM((4, S, T), BF16),
            pltpu.VMEM((2, S, T), BF16),
            pltpu.VMEM((2, S, T), BF16),
            pltpu.VMEM((2, T, 128), F32),
            pltpu.VMEM((2, T, 128), F32),
            pltpu.VMEM((T, S), BF16),
            pltpu.VMEM((T, S), BF16),
            pltpu.VMEM((T, S), BF16),
            pltpu.VMEM((T, S), BF16),
            pltpu.VMEM((S, T), F32),
            pltpu.VMEM((2, T, 128), F32),
            pltpu.VMEM((2, BLK, 128), F32),
            pltpu.VMEM((2, 2, BLK, 128), F32),
            pltpu.VMEM((2, SUB, 128), F32),
            pltpu.VMEM((2, 2, SUB, 128), F32),
            pltpu.VMEM((2, SUB, 128), F32),
            pltpu.VMEM((2, 4, 4, 8, W), F32),
            pltpu.VMEM((4, 4, 8, W), F32),
            pltpu.VMEM((2, 2, 8, W), F32),
            pltpu.VMEM((2, 4, 8, W), F32),
            pltpu.VMEM((2, 8, 768), F32),
            pltpu.VMEM((2, 8, W), F32),
            pltpu.VMEM((4, 8, S), F32),
            pltpu.SemaphoreType.DMA((N_COPIES,)),
            pltpu.SemaphoreType.DMA((N_COPIES,)),
            pltpu.SemaphoreType.DMA((6,)),
        ],
        compiler_params=pltpu.CompilerParams(
            collective_id=0, has_side_effects=True, vmem_limit_bytes=60 << 20
        ),
    )(weights, tile, lower, upper, pivot)


def body(
    inverse_tile, lower_factor, upper_factor, pivot_inverse, pole_weights, block_owners,
    basis_ancestor, basis_super,
):
    pole, row, col = lax.axis_index("pole"), lax.axis_index("row"), lax.axis_index("col")
    me = (pole * 4 + row) * 4 + col
    group = row * 32 + (pole % 4) * 8 + col * 2 + pole // 4

    owners = block_owners.T
    here = lax.dynamic_slice_in_dim(owners, group * NB, NB, 1)
    everyone = jnp.arange(DEV, dtype=jnp.int32)
    named = jnp.max((here[:, :, None] == everyone[None, None, :]).astype(F32), 0)
    before = (jnp.arange(NB)[:, None] > jnp.arange(NB)[None, :]).astype(F32)
    rank = jnp.dot(before, named)
    chosen = jnp.stack([named * (rank == slot) for slot in range(2)], 2).reshape(NB, 2 * DEV)

    mine = jnp.max((owners == me).astype(F32), 0).reshape(DEV, NB)
    place = jnp.dot(mine, before.T)
    ids = jnp.arange(DEV * NB, dtype=jnp.int32).reshape(DEV, NB)
    picked = jnp.stack(
        [jnp.sum(jnp.where((mine > 0) & (place == slot), ids, 0), 1) for slot in range(2)], 1
    )
    picked = picked.reshape(4, 4, 4, 2, 2).transpose(3, 1, 0, 2, 4).reshape(-1)
    row_ids = (picked[:, None] * 2 + jnp.arange(2, dtype=jnp.int32)[None, :]).reshape(-1)
    ancestor_rows = jnp.take(basis_ancestor, row_ids, axis=0, mode="clip")

    upper_density, lower_rows, pivot_rows = dense_part(
        pole_weights, inverse_tile, lower_factor, upper_factor, pivot_inverse
    )
    values = lax.dynamic_slice_in_dim(lower_rows, (pole // 4) * 36, 36, 0).reshape(NB, 2 * S)
    packed = lax.dot_general(
        chosen, values, (((0,), (0,)), ((), ())),
        precision=lax.Precision.HIGHEST, preferred_element_type=F32,
    ).reshape(DEV, 2, 2 * S)
    pivot_part = lax.dynamic_slice_in_dim(pivot_rows, col * 2, 2, 0).reshape(1, 1, 2 * S)
    packed = jnp.concatenate([packed, jnp.broadcast_to(pivot_part, (DEV, 1, 2 * S))], 1)
    got = lax.all_to_all(packed, ("pole", "row", "col"), split_axis=0, concat_axis=0, tiled=True)
    received = got[:, :2].reshape(-1, S)
    pivot_density = got[:, 2].reshape(S, S)
    high = lax.Precision.HIGH
    projected = jnp.dot(received, basis_super, precision=high, preferred_element_type=F32)
    charge = jnp.sum(ancestor_rows * projected, 0) + jnp.sum(
        basis_super
        * jnp.dot(pivot_density, basis_super, precision=high, preferred_element_type=F32),
        0,
    )
    return (upper_density, charge)


def solution(mesh):
    placed = (
        P("pole", None, "row", "col"),
        P("pole", None, "row", "col"),
        P("pole", None, "col", "row"),
        P("pole", None, "row", "col"),
        P("pole", None),
        P(),
        P(None, ("pole", "row", "col")),
        P(None, ("pole", "row", "col")),
    )
    return jax.shard_map(
        body,
        mesh=mesh,
        in_specs=placed,
        out_specs=(P(("pole", "row"), "col"), P(("pole", "row", "col"))),
        check_vma=False,
    )
```

```python
import jax
import jax.numpy as jnp
from jax import lax
from jax.experimental import pallas as pl
from jax.experimental.pallas import tpu as pltpu
from jax.sharding import PartitionSpec as P

MESH = pl.DeviceIdType.MESH
F32 = jnp.float32
BF16 = jnp.bfloat16
T = 1152
S = 256
Q = 64
NB = 18
TOPK = 6
BAT = 8
WIDE = 288
DEV = 128
CHUNKS = ((0, 512), (512, 512), (1024, 128))
BLK = 288
SUB = 72
FIRST = 40
LEFT = 640


def nt(a, b):
    return lax.dot_general(a, b, (((1,), (1,)), ((), ())), preferred_element_type=F32)


def nn(a, b):
    return jnp.dot(a, b, preferred_element_type=F32)


def split(v):
    hi = v.astype(BF16)
    return hi, (v - hi.astype(F32)).astype(BF16)


def tn(a, b):
    return lax.dot_general(a, b, (((0,), (0,)), ((), ())), preferred_element_type=F32)


def iota(shape, dim):
    return lax.broadcasted_iota(jnp.int32, shape, dim)


def rows_of(start, size):
    return pl.ds(pl.multiple_of(start, 8), size)


def kernel(
    w_ref, a_hbm, l_hbm, u_hbm, piv_ref, own_ref, bs_ref, ba_hbm,
    upper_out, charge_out,
    a32, ah, al, lf, uf, relay, bl, br, uph, upl, xr, xi, xih, xil, xrh, xrl, y, lt,
    rz1, rz2, ry1, ry2, rx, ld, cb, rc, ru1, ru2, rv1, rv2,
    pvb, pc, pz, px, pb, pfull, bsp, ba, ba8, sel, pk, got,
    sends, recvs, locs, asend, arecv,
):
    pole, row, col = lax.axis_index("pole"), lax.axis_index("row"), lax.axis_index("col")
    x_lo, z = pole // 4, pole % 4
    x_hi, core = row // 2, row % 2
    x = x_hi * 2 + x_lo
    me = (pole * 4 + row) * 4 + col
    group = row * 32 + z * 8 + col * 2 + x_lo

    def at_x(v):
        return ((v % 2) * 4 + z, (v // 2) * 2 + core, col)

    def at_y(v):
        return (pole, row, v)

    def at_z(v):
        return (x_lo * 4 + v, row, col)

    def row_x(v):
        return (v // 2) * 2 + core

    xp, xm, x2 = (x + 1) % 4, (x + 3) % 4, (x + 2) % 4
    yp, ym, y2 = (col + 1) % 4, (col + 3) % 4, (col + 2) % 4
    zp, zm, z2 = (z + 1) % 4, (z + 3) % 4, (z + 2) % 4
    d_core = (pole, x_hi * 2 + 1 - core, col)
    d_xp, d_xm = at_x(xp), at_x(xm)
    d_yp, d_ym = at_y(yp), at_y(ym)
    d_zp, d_zm = at_z(zp), at_z(zm)
    d_xn = at_x(x_hi * 2 + 1 - x_lo)
    started = []

    def send(src, dst, dev):
        n = len(started)
        c = pltpu.make_async_remote_copy(
            src_ref=src, dst_ref=dst, send_sem=sends.at[n], recv_sem=recvs.at[n],
            device_id=dev, device_id_type=MESH,
        )
        c.start()
        started.append(c)
        return c

    local_a = []
    for b in range(4):
        rs = slice(b * BLK, (b + 1) * BLK)
        c = pltpu.make_async_copy(a_hbm.at[0, :, rs, :], a32.at[:, rs, :], locs.at[b])
        local_a.append(c)
    local_l = pltpu.make_async_copy(l_hbm.at[0], lf.at[row], locs.at[4])
    local_u = pltpu.make_async_copy(u_hbm.at[0], uf.at[col], locs.at[5])
    local_ba = pltpu.make_async_copy(ba_hbm, ba, locs.at[6])
    local_l.start()
    local_a[0].start()
    local_a[1].start()

    barrier = pltpu.get_barrier_semaphore()
    greet = (d_core, d_xp, d_xm, at_x(x2), d_yp, d_ym, at_y(y2), d_zp, d_zm, at_z(z2))
    for dev in greet:
        pl.semaphore_signal(barrier, inc=1, device_id=dev, device_id_type=MESH)
    pl.semaphore_wait(barrier, len(greet))

    def lanes(k):
        return pl.ds(CHUNKS[k][0], CHUNKS[k][1])

    def l_own(k):
        return (
            send(l_hbm.at[0, 0, :, lanes(k)], relay.at[0, :, lanes(k)], d_xp),
            send(l_hbm.at[0, 1, :, lanes(k)], relay.at[1, :, lanes(k)], d_xm),
        )

    def l_relay(k, own):
        own[0].wait_recv()
        p = send(relay.at[0, :, lanes(k)], lf.at[row_x(xm), 0, :, lanes(k)], d_xp)
        own[1].wait_recv()
        m = send(relay.at[1, :, lanes(k)], lf.at[row_x(xp), 1, :, lanes(k)], d_xm)
        return p, m

    far = (1 - x_hi) * 2 + core

    def l_share(k, pair):
        pair[0].wait_recv()
        pair[1].wait_recv()
        return send(lf.at[far, :, :, lanes(k)], lf.at[far, :, :, lanes(k)], d_core)

    def u_own(k):
        return (
            send(u_hbm.at[0, :, :, lanes(k)], uf.at[col, :, :, lanes(k)], d_yp),
            send(u_hbm.at[0, :, :, lanes(k)], uf.at[col, :, :, lanes(k)], d_ym),
        )

    def u_forward(k, own):
        own[0].wait_recv()
        p = send(uf.at[ym, 0, :, lanes(k)], uf.at[ym, 0, :, lanes(k)], d_yp)
        own[1].wait_recv()
        m = send(uf.at[yp, 1, :, lanes(k)], uf.at[yp, 1, :, lanes(k)], d_ym)
        return p, m

    l_near = send(l_hbm.at[0], lf.at[row], d_core)
    lo = [l_own(0)]
    uo = [u_own(0)]
    lo.append(l_own(1))
    uo.append(u_own(1))
    local_a[2].start()
    local_a[3].start()
    local_u.start()
    local_ba.start()

    w_re, w_im = w_ref[0, 0], w_ref[0, 1]

    def build(dst, slot, q, lane):
        re, im = lf[slot, 0, :, lane], lf[slot, 1, :, lane]
        a, b = pl.ds(q * Q, Q), pl.ds(2 * Q + q * Q, Q)
        rh, rl = split(re)
        ih, il = split(im)
        dst[0, a, lane], dst[1, a, lane] = rh, rl
        dst[0, b, lane], dst[1, b, lane] = ih, il
        dst[2, a, lane], dst[3, a, lane] = -ih, -il
        dst[2, b, lane], dst[3, b, lane] = rh, rl

    def product(rs, lane, b):
        acc = nt(ah[0, rs, lane], b[0, :, lane])
        acc = acc + nt(ah[0, rs, lane], b[1, :, lane])
        acc = acc + nt(al[0, rs, lane], b[0, :, lane])
        acc = acc + nt(ah[1, rs, lane], b[2, :, lane])
        acc = acc + nt(ah[1, rs, lane], b[3, :, lane])
        acc = acc + nt(al[1, rs, lane], b[2, :, lane])
        return acc

    def split_a(b):
        local_a[b].wait()

        @pl.loop(0, BLK // 16)
        def _(i):
            rs = pl.ds(pl.multiple_of(b * BLK + i * 16, 16), 16)
            for part in range(2):
                hi, low = split(a32[part, rs, :])
                ah[part, rs, :] = hi
                al[part, rs, :] = low

    whole = pl.ds(0, T)

    def near(b):
        rs = pl.ds(b * BLK, BLK)
        acc = product(rs, whole, bl)
        xr[x_hi, rs, :] = acc[:, :128]
        xi[x_hi, rs, :] = acc[:, 128:]

    halves = (x_hi, 1 - x_hi)

    def lower_term(n):
        h = halves[n]

        @pl.loop(0, 4)
        def _(b):
            rs = pl.ds(pl.multiple_of(b * BLK, 16), BLK)
            lt[h, rs, :] = -(w_re * xi[h, rs, :] + w_im * xr[h, rs, :])

    def z_at(b):
        return b * BLK

    def y_at(b):
        return z * BLK + b * SUB

    z_ring = (z_at, BLK, 144, (zp, zm, z2, z), (d_zp, d_zm), rz1, rz2)
    y_ring = (y_at, SUB, FIRST, (yp, ym, y2, col), (d_yp, d_ym), ry1, ry2)

    def ring1(n, ring):
        at, size, first, (p, m, two, own), (dp, dm), r1, r2 = ring
        h = halves[n]
        return (
            send(lt.at[h, rows_of(at(two), first), :], r1.at[n, pl.ds(0, first), :], dp),
            send(
                lt.at[h, rows_of(at(two) + first, size - first), :],
                r1.at[n, pl.ds(first, size - first), :], dm,
            ),
        )

    def ring2(n, ring, before):
        at, size, first, (p, m, two, own), (dp, dm), r1, r2 = ring
        h = halves[n]
        before[0].wait_recv()
        lt[h, rows_of(at(p), first), :] += r1[n, 0:first]
        a = send(lt.at[h, rows_of(at(p), size), :], r2.at[n, 0], dp)
        before[1].wait_recv()
        lt[h, rows_of(at(m) + first, size - first), :] += r1[n, first:size]
        return a, send(lt.at[h, rows_of(at(m), size), :], r2.at[n, 1], dm)

    def ring3(n, ring, before):
        at, size, first, (p, m, two, own), (dp, dm), r1, r2 = ring
        before[0].wait_recv()
        before[1].wait_recv()
        lt[halves[n], rows_of(at(own), size), :] += r2[n, 0] + r2[n, 1]

    def x_swap(n):
        return send(lt.at[halves[n], rows_of(y_at(col), SUB), :], rx.at[n], d_xn)

    def x_add(n, before):
        before.wait_recv()
        ld[halves[n]] = lt[halves[n], rows_of(y_at(col), SUB), :] + rx[n]

    def upper_chunk(k):
        lane = lanes(k)
        for q in range(4):
            re, im = uf[q, 0, :, lane], uf[q, 1, :, lane]
            rs = pl.ds(q * Q, Q)
            for part, v in ((0, w_re * re - w_im * im), (1, w_re * im + w_im * re)):
                hi, low = split(v)
                uph[part, rs, lane] = hi
                upl[part, rs, lane] = low
        acc = nn(uph[0, :, lane], ah[1, lane, :])
        acc = acc + nn(uph[0, :, lane], al[1, lane, :])
        acc = acc + nn(upl[0, :, lane], ah[1, lane, :])
        acc = acc + nn(uph[1, :, lane], ah[0, lane, :])
        acc = acc + nn(uph[1, :, lane], al[0, lane, :])
        acc = acc + nn(upl[1, :, lane], ah[0, lane, :])
        if k == 0:
            y[...] = acc
        else:
            y[...] += acc

    def far_chunk(k):
        for q in range(2):
            build(br, (1 - x_hi) * 2 + q, q, lanes(k))

        @pl.loop(0, 4)
        def _(b):
            rs = pl.ds(pl.multiple_of(b * BLK, 16), BLK)
            acc = product(rs, lanes(k), br)
            if k == 0:
                xr[1 - x_hi, rs, :] = acc[:, :128]
                xi[1 - x_hi, rs, :] = acc[:, 128:]
            else:
                xr[1 - x_hi, rs, :] += acc[:, :128]
                xi[1 - x_hi, rs, :] += acc[:, 128:]

    def choose_rows():
        mine = own_ref[group // 16].astype(F32).astype(BF16)
        here = nn(
            mine,
            (iota((WIDE, NB), 0) == (group % 16) * NB + iota((WIDE, NB), 1)).astype(F32).astype(BF16),
        )
        owner = iota((2 * DEV, NB), 0)
        named = jnp.zeros((2 * DEV, NB), F32)
        for t in range(TOPK):
            hit = here[t : t + 1, :] == (owner // 2).astype(F32)
            named = jnp.maximum(named, hit.astype(F32))
        earlier = (iota((NB, NB), 0) < iota((NB, NB), 1)).astype(F32).astype(BF16)
        rank = nn(named.astype(BF16), earlier)
        chosen = named * (rank == (owner % 2).astype(F32)).astype(F32)
        spot = iota((NB, 2 * SUB), 1) % SUB
        spread = (
            (spot // 36 == x_lo) & ((spot % 36) // 2 == iota((NB, 2 * SUB), 0))
        ).astype(F32)
        wide = nn(chosen.astype(BF16), spread.astype(BF16))
        out = iota((8 * DEV, 2 * DEV), 0)
        repeat = (iota((8 * DEV, 2 * DEV), 1) == (out // 8) * 2 + (out // 2) % 2).astype(F32)
        full = nn(repeat.astype(BF16), wide.astype(BF16))
        ro, co = iota((8 * DEV, 2 * SUB), 0), iota((8 * DEV, 2 * SUB), 1)
        keep = ((ro // 4) % 2 == co // SUB) & (ro % 2 == co % 2)
        sel[...] = jnp.where(keep, full, 0.0).astype(BF16)

    def choose_ancestors():
        local_ba.wait()
        block = iota((WIDE, WIDE), 0), iota((WIDE, WIDE), 1)
        earlier = ((block[0] // NB == block[1] // NB) & (block[0] < block[1])).astype(F32)
        earlier = earlier.astype(BF16)
        slot = iota((8 * 16, WIDE), 0)
        wanted = slot - (slot // 4) % 2 * 4 - slot % 2

        @pl.loop(0, BAT)
        def _(b):
            owners = own_ref[b]
            mine = jnp.max((owners == me).astype(F32), 0, keepdims=True)
            rank = nn(jnp.broadcast_to(mine, (8, WIDE)).astype(BF16), earlier)[0:1, :]
            base = (iota((1, WIDE), 1) // NB * 8).astype(F32)
            key = jnp.where(mine > 0, base + 2 * rank, -8.0)
            hit = key == wanted.astype(F32)
            acc = jnp.zeros((8 * 16, 128), F32)
            for parity in range(2):
                one = (hit & (slot % 2 == parity)).astype(F32).astype(BF16)
                v = ba[pl.ds(b * 2 * WIDE + parity, WIDE, stride=2), :]
                hi, low = split(v)
                acc = acc + nn(one, hi) + nn(one, low)
            ba8[rows_of(b * 128, 128), :] = acc

    def exchange():
        v = ld[...].reshape(2 * SUB, 128)
        hi, low = split(v)
        rest = (v - hi.astype(F32) - low.astype(F32)).astype(BF16)
        packed = nn(sel[...], hi) + nn(sel[...], low) + nn(sel[...], rest)
        pk[...] = packed.reshape(DEV, 8, 128)
        got[group] = pk[me]

        @pl.loop(1, DEV)
        def _(d):
            t = (me + d) % DEV
            pltpu.make_async_remote_copy(
                src_ref=pk.at[t], dst_ref=got.at[group], send_sem=asend.at[0], recv_sem=arecv.at[0],
                device_id=(t // 16, (t // 4) % 4, t % 4), device_id_type=MESH,
            ).start()

    def three(a, b):
        ahi, alo = split(a)
        bhi, blo = split(b)
        return nn(ahi, bhi) + nn(ahi, blo) + nn(alo, bhi)

    local_l.wait()
    l_near.wait_recv()
    for q in range(2):
        build(bl, x_hi * 2 + q, q, whole)
    split_a(0)
    near(0)
    split_a(1)
    lr = [l_relay(0, lo[0])]
    lo.append(l_own(2))
    near(1)
    split_a(2)
    lr.append(l_relay(1, lo[1]))
    uf_moves = [u_forward(0, uo[0])]
    uo.append(u_own(2))
    near(2)
    ls = [l_share(0, lr[0])]
    lr.append(l_relay(2, lo[2]))
    split_a(3)
    near(3)
    lower_term(0)
    zn = ring1(0, z_ring)
    ls.append(l_share(1, lr[1]))
    ls[0].wait_recv()
    far_chunk(0)
    zn = ring2(0, z_ring, zn)
    uf_moves.append(u_forward(1, uo[1]))
    ls.append(l_share(2, lr[2]))
    ls[1].wait_recv()
    far_chunk(1)
    uf_moves.append(u_forward(2, uo[2]))
    ring3(0, z_ring, zn)
    yn = ring1(0, y_ring)
    ls[2].wait_recv()
    far_chunk(2)
    lower_term(1)
    zf = ring1(1, z_ring)
    local_u.wait()
    for h in range(2):
        hs = pl.ds(h * 128, 128)
        hi, low = split(xi[h])
        xih[:, hs], xil[:, hs] = hi, low
        hi, low = split(xr[h])
        xrh[:, hs], xrl[:, hs] = hi, low
    for c in uf_moves[0]:
        c.wait_recv()
    zf = ring2(1, z_ring, zf)
    yn = ring2(0, y_ring, yn)
    upper_chunk(0)
    ring3(0, y_ring, yn)
    xn = x_swap(0)
    for c in uf_moves[1]:
        c.wait_recv()
    upper_chunk(1)
    ring3(1, z_ring, zf)
    yf = ring1(1, y_ring)
    x_add(0, xn)
    for c in uf_moves[2]:
        c.wait_recv()
    upper_chunk(2)

    for g in range(32):
        at = (g % 2, (g // 4) % 4, ((g // 2) % 2) * 2 + g // 16)
        cb[at[0], at[1], at[2]] = -y[g * 8 : g * 8 + 8, :]
    to_core = send(cb.at[1 - core], rc, d_core)

    pv = nn(uph[0], xih[...])
    pv = pv + nn(uph[0], xil[...])
    pv = pv + nn(upl[0], xih[...])
    pv = pv + nn(uph[1], xrh[...])
    pv = pv + nn(uph[1], xrl[...])
    pv = pv + nn(upl[1], xrh[...])
    place = (iota((Q, S), 1) == iota((Q, S), 0) + col * Q).astype(F32)
    piece = w_re * piv_ref[0, 1] + w_im * piv_ref[0, 0]
    placed = jnp.dot(piece, place, precision=lax.Precision.HIGHEST, preferred_element_type=F32)
    for g in range(32):
        at = (g % 2, (g // 4) % 4, ((g // 2) % 2) * 2 + g // 16)
        mine = (row == g // 8).astype(F32)
        pvb[at[0], at[1], at[2]] = (
            pv[g * 8 : g * 8 + 8, :] + mine * placed[(g % 8) * 8 : (g % 8) * 8 + 8, :]
        )
    p1 = send(pvb.at[1 - core], pc, d_core)
    yf = ring2(1, y_ring, yf)

    to_core.wait_recv()

    @pl.loop(0, 4)
    def _(b):
        cb[core, b] += rc[b]

    f1p = send(cb.at[core, z2, pl.ds(0, 2)], ru1.at[0], d_zp)
    f1m = send(cb.at[core, z2, pl.ds(2, 2)], ru1.at[1], d_zm)
    p1.wait_recv()
    pvb[core] += pc[...]
    p2 = [
        send(pvb.at[core, (z + d) % 4], pz.at[d - 1], at_z((z + d) % 4)) for d in range(1, 4)
    ]
    choose_rows()
    ring3(1, y_ring, yf)
    xf = x_swap(1)
    for g in range(32):
        k = (g % 2) * 16 + ((g // 4) % 4) * 4 + ((g // 2) % 2) * 2 + g // 16
        bsp[k * 8 : k * 8 + 8, :] = bs_ref[g * 8 : g * 8 + 8, :]

    for c in p2:
        c.wait_recv()
    pvb[core, z] += pz[0] + pz[1] + pz[2]
    p3 = [
        send(pvb.at[core, z, (x + d) % 4], px.at[d - 1], at_x((x + d) % 4)) for d in range(1, 4)
    ]
    x_add(1, xf)
    exchange()
    f1p.wait_recv()
    cb[core, zp, 0:2] += ru1[0]
    f2p = send(cb.at[core, zp], ru2.at[0], d_zp)
    f1m.wait_recv()
    cb[core, zm, 2:4] += ru1[1]
    f2m = send(cb.at[core, zm], ru2.at[1], d_zm)
    for c in p3:
        c.wait_recv()
    pb[col] = pvb[core, z, x] + px[0] + px[1] + px[2]
    p4 = [send(pb.at[col], pb.at[col], at_y((col + d) % 4)) for d in range(1, 4)]
    choose_ancestors()
    for c in p4:
        c.wait_recv()
    pfull[core, z, x] = pb[0] + pb[1] + pb[2] + pb[3]
    p5 = [
        send(pfull.at[core, z, x], pfull.at[core, z, x], at_x((x + d) % 4)) for d in range(1, 4)
    ]
    f2p.wait_recv()
    f2m.wait_recv()
    cb[core, z] += ru2[0] + ru2[1]
    rest = T - LEFT
    h1p = send(cb.at[core, z, x2, :, pl.ds(0, LEFT)], rv1.at[0], d_xp)
    h1m = send(cb.at[core, z, x2, :, pl.ds(LEFT, rest)], rv1.at[1, :, pl.ds(0, rest)], d_xm)
    for c in p5:
        c.wait_recv()
    p6 = [
        send(pfull.at[core, z], pfull.at[core, z], at_z((z + d) % 4)) for d in range(1, 4)
    ]
    h1p.wait_recv()
    cb[core, z, xp, :, :LEFT] += rv1[0]
    h2p = send(cb.at[core, z, xp], rv2.at[0], d_xp)
    h1m.wait_recv()
    cb[core, z, xm, :, LEFT:] += rv1[1, :, :rest]
    h2m = send(cb.at[core, z, xm], rv2.at[1], d_xm)
    for c in p6:
        c.wait_recv()
    p7 = send(pfull.at[core], pfull.at[core], d_core)

    pltpu.make_async_copy(got.at[pl.ds(0, DEV - 1)], got.at[pl.ds(0, DEV - 1)], arecv.at[0]).wait()
    received = got[...].reshape(8 * DEV, 128)
    both = jnp.concatenate([bs_ref[0:128, :], bs_ref[128:256, :]], 1)
    projected = three(received, both)
    first = (iota((8 * DEV, 128), 0) // 4) % 2 == 0
    projected = jnp.where(first, projected[:, :128], projected[:, 128:])
    charge = jnp.sum(ba8[...] * projected, 0, keepdims=True)
    h2p.wait_recv()
    h2m.wait_recv()
    upper_out[...] = cb[core, z, x] + rv2[0] + rv2[1]
    p7.wait_recv()
    pivot = pfull[...].reshape(S, S)
    charge_out[...] = charge + jnp.sum(bsp[...] * three(pivot, bs_ref[...]), 0, keepdims=True)
    pltpu.make_async_copy(pk.at[pl.ds(0, DEV - 1)], pk.at[pl.ds(0, DEV - 1)], asend.at[0]).wait()
    for c in started:
        c.wait_send()


N_COPIES = 80


def fused(weights, tile, lower, upper, pivot, owners, basis_super, basis_ancestor):
    vmem = pl.BlockSpec(memory_space=pltpu.VMEM)
    hbm = pl.BlockSpec(memory_space=pl.ANY)
    return pl.pallas_call(
        kernel,
        out_shape=(jax.ShapeDtypeStruct((8, T), F32), jax.ShapeDtypeStruct((1, 128), F32)),
        in_specs=[pl.BlockSpec(memory_space=pltpu.SMEM), hbm, hbm, hbm, vmem, vmem, vmem, hbm],
        out_specs=(vmem, vmem),
        scratch_shapes=[
            pltpu.VMEM((2, T, T), F32),
            pltpu.VMEM((2, T, T), BF16),
            pltpu.VMEM((2, T, T), BF16),
            pltpu.VMEM((4, 2, Q, T), F32),
            pltpu.VMEM((4, 2, Q, T), F32),
            pltpu.VMEM((2, Q, T), F32),
            pltpu.VMEM((4, S, T), BF16),
            pltpu.VMEM((4, S, T), BF16),
            pltpu.VMEM((2, S, T), BF16),
            pltpu.VMEM((2, S, T), BF16),
            pltpu.VMEM((2, T, 128), F32),
            pltpu.VMEM((2, T, 128), F32),
            pltpu.VMEM((T, S), BF16),
            pltpu.VMEM((T, S), BF16),
            pltpu.VMEM((T, S), BF16),
            pltpu.VMEM((T, S), BF16),
            pltpu.VMEM((S, T), F32),
            pltpu.VMEM((2, T, 128), F32),
            pltpu.VMEM((2, BLK, 128), F32),
            pltpu.VMEM((2, 2, BLK, 128), F32),
            pltpu.VMEM((2, SUB, 128), F32),
            pltpu.VMEM((2, 2, SUB, 128), F32),
            pltpu.VMEM((2, SUB, 128), F32),
            pltpu.VMEM((2, SUB, 128), F32),
            pltpu.VMEM((2, 4, 4, 8, T), F32),
            pltpu.VMEM((4, 4, 8, T), F32),
            pltpu.VMEM((2, 2, 8, T), F32),
            pltpu.VMEM((2, 4, 8, T), F32),
            pltpu.VMEM((2, 8, LEFT), F32),
            pltpu.VMEM((2, 8, T), F32),
            pltpu.VMEM((2, 4, 4, 8, S), F32),
            pltpu.VMEM((4, 4, 8, S), F32),
            pltpu.VMEM((3, 4, 8, S), F32),
            pltpu.VMEM((3, 8, S), F32),
            pltpu.VMEM((4, 8, S), F32),
            pltpu.VMEM((2, 4, 4, 8, S), F32),
            pltpu.VMEM((S, 128), F32),
            pltpu.VMEM((4608, 128), F32),
            pltpu.VMEM((8 * DEV, 128), F32),
            pltpu.VMEM((8 * DEV, 2 * SUB), BF16),
            pltpu.VMEM((DEV, 8, 128), F32),
            pltpu.VMEM((DEV, 8, 128), F32),
            pltpu.SemaphoreType.DMA((N_COPIES,)),
            pltpu.SemaphoreType.DMA((N_COPIES,)),
            pltpu.SemaphoreType.DMA((7,)),
            pltpu.SemaphoreType.DMA((1,)),
            pltpu.SemaphoreType.DMA((1,)),
        ],
        compiler_params=pltpu.CompilerParams(
            collective_id=0, has_side_effects=True, vmem_limit_bytes=63 << 20
        ),
    )(weights, tile, lower, upper, pivot, owners, basis_super, basis_ancestor)


def body(
    inverse_tile, lower_factor, upper_factor, pivot_inverse, pole_weights, block_owners,
    basis_ancestor, basis_super,
):
    owners = block_owners.T.reshape(TOPK, BAT, WIDE).transpose(1, 0, 2)
    upper_density, charge = fused(
        pole_weights, inverse_tile, lower_factor, upper_factor, pivot_inverse, owners, basis_super,
        basis_ancestor,
    )
    return (upper_density, charge.reshape(128))


def solution(mesh):
    placed = (
        P("pole", None, "row", "col"),
        P("pole", None, "row", "col"),
        P("pole", None, "col", "row"),
        P("pole", None, "row", "col"),
        P("pole", None),
        P(),
        P(None, ("pole", "row", "col")),
        P(None, ("pole", "row", "col")),
    )
    return jax.shard_map(
        body,
        mesh=mesh,
        in_specs=placed,
        out_specs=(P(("pole", "row"), "col"), P(("pole", "row", "col"))),
        check_vma=False,
    )
```

```python
import jax
import jax.numpy as jnp
from jax import lax
from jax.experimental import pallas as pl
from jax.experimental.pallas import tpu as pltpu
from jax.sharding import PartitionSpec as P

MESH = pl.DeviceIdType.MESH
F32 = jnp.float32
BF16 = jnp.bfloat16
T = 1152
S = 256
Q = 64
NB = 18
TOPK = 6
BAT = 8
WIDE = 288
DEV = 128
CHUNKS = ((0, 512), (512, 512), (1024, 128))
BLK = 288
SUB = 72
FIRST = 40
TAIL = 1024
LEFT = 640


def nt(a, b):
    return lax.dot_general(a, b, (((1,), (1,)), ((), ())), preferred_element_type=F32)


def nn(a, b):
    return jnp.dot(a, b, preferred_element_type=F32)


def split(v):
    hi = v.astype(BF16)
    return hi, (v - hi.astype(F32)).astype(BF16)


def tn(a, b):
    return lax.dot_general(a, b, (((0,), (0,)), ((), ())), preferred_element_type=F32)


def iota(shape, dim):
    return lax.broadcasted_iota(jnp.int32, shape, dim)


def rows_of(start, size):
    return pl.ds(pl.multiple_of(start, 8), size)


def kernel(
    w_ref, a_hbm, l_hbm, u_hbm, piv_ref, own_ref, bs_ref, ba_hbm,
    out_ref,
    a32, ah, al, lf, uf, relay, bl, br, uph, upl, xr, xi, xih, xil, xrh, xrl, y, lt,
    rz1, rz2, ry1, ry2, rx, ld, cb, rc, ru1, ru2, rv1, rv2,
    pvb, pc, pz, pb, pfull, bsp, ba, ba8, sel, pk, got, own_s, pvs, ath, atl, bt,
    sends, recvs, locs, asend, arecv,
):
    pole, row, col = lax.axis_index("pole"), lax.axis_index("row"), lax.axis_index("col")
    x_lo, z = pole // 4, pole % 4
    x_hi, core = row // 2, row % 2
    x = x_hi * 2 + x_lo
    me = (pole * 4 + row) * 4 + col
    group = row * 32 + z * 8 + col * 2 + x_lo

    def at_x(v):
        return ((v % 2) * 4 + z, (v // 2) * 2 + core, col)

    def at_y(v):
        return (pole, row, v)

    def at_z(v):
        return (x_lo * 4 + v, row, col)

    def row_x(v):
        return (v // 2) * 2 + core

    xp, xm, x2 = (x + 1) % 4, (x + 3) % 4, (x + 2) % 4
    yp, ym, y2 = (col + 1) % 4, (col + 3) % 4, (col + 2) % 4
    zp, zm, z2 = (z + 1) % 4, (z + 3) % 4, (z + 2) % 4
    d_core = (pole, x_hi * 2 + 1 - core, col)
    d_xp, d_xm = at_x(xp), at_x(xm)
    d_yp, d_ym = at_y(yp), at_y(ym)
    d_zp, d_zm = at_z(zp), at_z(zm)
    d_xn = at_x(x_hi * 2 + 1 - x_lo)
    started = []

    def send(src, dst, dev):
        n = len(started)
        c = pltpu.make_async_remote_copy(
            src_ref=src, dst_ref=dst, send_sem=sends.at[n], recv_sem=recvs.at[n],
            device_id=dev, device_id_type=MESH,
        )
        c.start()
        started.append(c)
        return c

    local_a = []
    for b in range(4):
        rs = slice(b * BLK, (b + 1) * BLK)
        c = pltpu.make_async_copy(a_hbm.at[0, :, rs, :], a32.at[:, rs, :], locs.at[b])
        local_a.append(c)
    local_l = pltpu.make_async_copy(l_hbm.at[0], lf.at[row], locs.at[4])
    local_u = pltpu.make_async_copy(u_hbm.at[0], uf.at[col], locs.at[5])
    local_ba = pltpu.make_async_copy(ba_hbm, ba, locs.at[6])
    local_l.start()
    for c in local_a:
        c.start()

    def split_a(b):
        local_a[b].wait()

        @pl.loop(0, BLK // 16)
        def _(i):
            rs = pl.ds(pl.multiple_of(b * BLK + i * 16, 16), 16)
            for part in range(2):
                hi, low = split(a32[part, rs, :])
                ah[part, rs, :] = hi
                al[part, rs, :] = low
                ath[rs, part * 128 : part * 128 + 128] = hi[:, TAIL:]
                atl[rs, part * 128 : part * 128 + 128] = low[:, TAIL:]

    barrier = pltpu.get_barrier_semaphore()
    greet = (d_core, d_xp, d_xm, d_yp, d_ym, d_zp, d_zm)
    for dev in greet:
        pl.semaphore_signal(barrier, inc=1, device_id=dev, device_id_type=MESH)
    split_a(0)
    pl.semaphore_wait(barrier, len(greet))

    def lanes(k):
        return pl.ds(CHUNKS[k][0], CHUNKS[k][1])

    def l_own(k):
        return (
            send(l_hbm.at[0, 0, :, lanes(k)], relay.at[0, :, lanes(k)], d_xp),
            send(l_hbm.at[0, 1, :, lanes(k)], relay.at[1, :, lanes(k)], d_xm),
        )

    def l_relay(k, own):
        own[0].wait_recv()
        p = send(relay.at[0, :, lanes(k)], lf.at[row_x(xm), 0, :, lanes(k)], d_xp)
        own[1].wait_recv()
        m = send(relay.at[1, :, lanes(k)], lf.at[row_x(xp), 1, :, lanes(k)], d_xm)
        return p, m

    far = (1 - x_hi) * 2 + core

    def l_share(k, pair):
        pair[0].wait_recv()
        pair[1].wait_recv()
        return send(lf.at[far, :, :, lanes(k)], lf.at[far, :, :, lanes(k)], d_core)

    def u_own(k):
        return (
            send(u_hbm.at[0, :, :, lanes(k)], uf.at[col, :, :, lanes(k)], d_yp),
            send(u_hbm.at[0, :, :, lanes(k)], uf.at[col, :, :, lanes(k)], d_ym),
        )

    def u_forward(k, own):
        own[0].wait_recv()
        p = send(uf.at[ym, 0, :, lanes(k)], uf.at[ym, 0, :, lanes(k)], d_yp)
        own[1].wait_recv()
        m = send(uf.at[yp, 1, :, lanes(k)], uf.at[yp, 1, :, lanes(k)], d_ym)
        return p, m

    l_near, lo, uo = [], [], []
    for k in range(3):
        l_near.append(send(l_hbm.at[0, :, :, lanes(k)], lf.at[row, :, :, lanes(k)], d_core))
        lo.append(l_own(k))
        uo.append(u_own(k))
    local_ba.start()
    local_u.start()

    w_re, w_im = w_ref[0, 0], w_ref[0, 1]

    def build(dst, slot, q, lane):
        re, im = lf[slot, 0, :, lane], lf[slot, 1, :, lane]
        a, b = pl.ds(q * Q, Q), pl.ds(2 * Q + q * Q, Q)
        rh, rl = split(re)
        ih, il = split(im)
        if lane.start == TAIL:
            one, two = pl.ds(0, 128), pl.ds(128, 128)
            bt[0, a, one], bt[1, a, one] = rh, rl
            bt[0, b, one], bt[1, b, one] = ih, il
            bt[0, a, two], bt[1, a, two] = -ih, -il
            bt[0, b, two], bt[1, b, two] = rh, rl
            return
        dst[0, a, lane], dst[1, a, lane] = rh, rl
        dst[0, b, lane], dst[1, b, lane] = ih, il
        dst[2, a, lane], dst[3, a, lane] = -ih, -il
        dst[2, b, lane], dst[3, b, lane] = rh, rl

    def product(rs, lane, b):
        acc = nt(ah[0, rs, lane], b[0, :, lane])
        acc = acc + nt(ah[0, rs, lane], b[1, :, lane])
        acc = acc + nt(al[0, rs, lane], b[0, :, lane])
        acc = acc + nt(ah[1, rs, lane], b[2, :, lane])
        acc = acc + nt(ah[1, rs, lane], b[3, :, lane])
        acc = acc + nt(al[1, rs, lane], b[2, :, lane])
        return acc

    halves = (x_hi, 1 - x_hi)

    def lower_term(n):
        h = halves[n]

        @pl.loop(0, 4)
        def _(b):
            rs = pl.ds(pl.multiple_of(b * BLK, 16), BLK)
            lt[h, rs, :] = -(w_re * xi[h, rs, :] + w_im * xr[h, rs, :])

    def z_at(b):
        return b * BLK

    def y_at(b):
        return z * BLK + b * SUB

    z_ring = (z_at, BLK, 144, (zp, zm, z2, z), (d_zp, d_zm), rz1, rz2)
    y_ring = (y_at, SUB, FIRST, (yp, ym, y2, col), (d_yp, d_ym), ry1, ry2)

    def ring1(n, ring):
        at, size, first, (p, m, two, own), (dp, dm), r1, r2 = ring
        h = halves[n]
        return (
            send(lt.at[h, rows_of(at(two), first), :], r1.at[n, pl.ds(0, first), :], dp),
            send(
                lt.at[h, rows_of(at(two) + first, size - first), :],
                r1.at[n, pl.ds(first, size - first), :], dm,
            ),
        )

    def ring2(n, ring, before):
        at, size, first, (p, m, two, own), (dp, dm), r1, r2 = ring
        h = halves[n]
        before[0].wait_recv()
        lt[h, rows_of(at(p), first), :] += r1[n, 0:first]
        a = send(lt.at[h, rows_of(at(p), size), :], r2.at[n, 0], dp)
        before[1].wait_recv()
        lt[h, rows_of(at(m) + first, size - first), :] += r1[n, first:size]
        return a, send(lt.at[h, rows_of(at(m), size), :], r2.at[n, 1], dm)

    def ring3(n, ring, before):
        at, size, first, (p, m, two, own), (dp, dm), r1, r2 = ring
        before[0].wait_recv()
        before[1].wait_recv()
        lt[halves[n], rows_of(at(own), size), :] += r2[n, 0] + r2[n, 1]

    def x_swap(n):
        return send(lt.at[halves[n], rows_of(y_at(col), SUB), :], rx.at[n], d_xn)

    def x_add(n, before):
        before.wait_recv()
        ld[halves[n]] = lt[halves[n], rows_of(y_at(col), SUB), :] + rx[n]

    def upper_prep(k):
        lane = lanes(k)
        for q in range(4):
            re, im = uf[q, 0, :, lane], uf[q, 1, :, lane]
            rs = pl.ds(q * Q, Q)
            for part, v in ((0, w_re * re - w_im * im), (1, w_re * im + w_im * re)):
                hi, low = split(v)
                uph[part, rs, lane] = hi
                upl[part, rs, lane] = low

    def upper_chunk(k):
        lane = lanes(k)
        acc = nn(uph[0, :, lane], ah[1, lane, :])
        acc = acc + nn(uph[0, :, lane], al[1, lane, :])
        acc = acc + nn(upl[0, :, lane], ah[1, lane, :])
        acc = acc + nn(uph[1, :, lane], ah[0, lane, :])
        acc = acc + nn(uph[1, :, lane], al[0, lane, :])
        acc = acc + nn(upl[1, :, lane], ah[0, lane, :])
        if k == 0:
            y[...] = acc
        else:
            y[...] += acc

    def chunk(n, k, blocks=(0, 4)):
        dst, h = ((bl, br)[n], halves[n])
        if blocks[0] == 0:
            for q in range(2):
                build(dst, h * 2 + q, q, lanes(k))

        @pl.loop(*blocks)
        def _(b):
            rs = pl.ds(pl.multiple_of(b * BLK, 16), BLK)
            if k == 2:
                acc = nt(ath[rs, :], bt[0]) + nt(ath[rs, :], bt[1]) + nt(atl[rs, :], bt[0])
            else:
                acc = product(rs, lanes(k), dst)
            if k == 0:
                xr[h, rs, :] = acc[:, :128]
                xi[h, rs, :] = acc[:, 128:]
            else:
                xr[h, rs, :] += acc[:, :128]
                xi[h, rs, :] += acc[:, 128:]

    def pivot_chunk(k):
        lane = lanes(k)
        acc = nn(uph[0, :, lane], xih[lane, :])
        acc = acc + nn(uph[0, :, lane], xil[lane, :])
        acc = acc + nn(upl[0, :, lane], xih[lane, :])
        acc = acc + nn(uph[1, :, lane], xrh[lane, :])
        acc = acc + nn(uph[1, :, lane], xrl[lane, :])
        acc = acc + nn(upl[1, :, lane], xrh[lane, :])
        if k == 0:
            pvs[...] = acc
        else:
            pvs[...] += acc

    def choose_rows():
        for b in range(BAT):
            own_s[b] = own_ref[:, b * WIDE : (b + 1) * WIDE]
        mine = own_s[group // 16].astype(F32).astype(BF16)
        here = nn(
            mine,
            (iota((WIDE, NB), 0) == (group % 16) * NB + iota((WIDE, NB), 1)).astype(F32).astype(BF16),
        )
        owner = iota((2 * DEV, NB), 0)
        named = jnp.zeros((2 * DEV, NB), F32)
        for t in range(TOPK):
            hit = here[t : t + 1, :] == (owner // 2).astype(F32)
            named = jnp.maximum(named, hit.astype(F32))
        earlier = (iota((NB, NB), 0) < iota((NB, NB), 1)).astype(F32).astype(BF16)
        rank = nn(named.astype(BF16), earlier)
        chosen = named * (rank == (owner % 2).astype(F32)).astype(F32)
        spot = iota((NB, 2 * SUB), 1) % SUB
        spread = (
            (spot // 36 == x_lo) & ((spot % 36) // 2 == iota((NB, 2 * SUB), 0))
        ).astype(F32)
        wide = nn(chosen.astype(BF16), spread.astype(BF16))
        out = iota((8 * DEV, 2 * DEV), 0)
        repeat = (iota((8 * DEV, 2 * DEV), 1) == (out // 8) * 2 + (out // 2) % 2).astype(F32)
        full = nn(repeat.astype(BF16), wide.astype(BF16))
        ro, co = iota((8 * DEV, 2 * SUB), 0), iota((8 * DEV, 2 * SUB), 1)
        keep = ((ro // 4) % 2 == co // SUB) & (ro % 2 == co % 2)
        sel[...] = jnp.where(keep, full, 0.0).astype(BF16)

    def choose_ancestors(start, stop):
        if start == 0:
            local_ba.wait()
        block = iota((WIDE, WIDE), 0), iota((WIDE, WIDE), 1)
        earlier = ((block[0] // NB == block[1] // NB) & (block[0] < block[1])).astype(F32)
        earlier = earlier.astype(BF16)
        slot = iota((8 * 16, WIDE), 0)
        wanted = slot - (slot // 4) % 2 * 4 - slot % 2

        @pl.loop(start, stop)
        def _(b):
            owners = own_s[b]
            mine = jnp.max((owners == me).astype(F32), 0, keepdims=True)
            rank = nn(jnp.broadcast_to(mine, (8, WIDE)).astype(BF16), earlier)[0:1, :]
            base = (iota((1, WIDE), 1) // NB * 8).astype(F32)
            key = jnp.where(mine > 0, base + 2 * rank, -8.0)
            hit = key == wanted.astype(F32)
            acc = jnp.zeros((8 * 16, 128), F32)
            for parity in range(2):
                one = (hit & (slot % 2 == parity)).astype(F32).astype(BF16)
                v = ba[pl.ds(b * 2 * WIDE + parity, WIDE, stride=2), :]
                hi, low = split(v)
                acc = acc + nn(one, hi) + nn(one, low)
            ba8[rows_of(b * 128, 128), :] = acc

    def exchange():
        v = ld[...].reshape(2 * SUB, 128)
        hi, low = split(v)
        rest = (v - hi.astype(F32) - low.astype(F32)).astype(BF16)
        packed = nn(sel[...], hi) + nn(sel[...], low) + nn(sel[...], rest)
        pk[...] = packed.reshape(DEV, 8, 128)
        got[group] = pk[me]

        for n in range(1, DEV):
            p, r, c = (pole + n // 16) % 8, (row + n // 4) % 4, (col + n) % 4
            pltpu.make_async_remote_copy(
                src_ref=pk.at[(p * 4 + r) * 4 + c], dst_ref=got.at[group],
                send_sem=asend.at[0], recv_sem=arecv.at[0],
                device_id=(p, r, c), device_id_type=MESH,
            ).start()

    def three(a, b):
        ahi, alo = split(a)
        bhi, blo = split(b)
        return nn(ahi, bhi) + nn(ahi, blo) + nn(alo, bhi)

    for b in range(1, 4):
        split_a(b)
    local_l.wait()
    l_near[0].wait_recv()
    chunk(0, 0)
    l_near[1].wait_recv()
    chunk(0, 1, (0, 2))
    lr = [l_relay(0, lo[0])]
    chunk(0, 1, (2, 4))
    l_near[2].wait_recv()
    chunk(0, 2)
    lower_term(0)
    zn = ring1(0, z_ring)
    lr.append(l_relay(1, lo[1]))
    lr.append(l_relay(2, lo[2]))
    uf_moves = [u_forward(0, uo[0])]
    choose_rows()
    choose_ancestors(0, 4)
    ls = [l_share(0, lr[0])]
    choose_ancestors(4, 8)
    zn = ring2(0, z_ring, zn)
    ls[0].wait_recv()
    chunk(1, 0, (0, 2))
    ls.append(l_share(1, lr[1]))
    uf_moves.append(u_forward(1, uo[1]))
    chunk(1, 0, (2, 4))
    ls.append(l_share(2, lr[2]))
    uf_moves.append(u_forward(2, uo[2]))
    ls[1].wait_recv()
    chunk(1, 1)
    ring3(0, z_ring, zn)
    yn = ring1(0, y_ring)
    ls[2].wait_recv()
    chunk(1, 2)
    lower_term(1)
    zf = ring1(1, z_ring)
    local_u.wait()
    for h in range(2):
        hs = pl.ds(h * 128, 128)
        hi, low = split(xi[h])
        xih[:, hs], xil[:, hs] = hi, low
        hi, low = split(xr[h])
        xrh[:, hs], xrl[:, hs] = hi, low
    for c in uf_moves[0]:
        c.wait_recv()
    upper_prep(0)
    upper_chunk(0)
    yn = ring2(0, y_ring, yn)
    pivot_chunk(0)
    zf = ring2(1, z_ring, zf)
    for c in uf_moves[1]:
        c.wait_recv()
    upper_prep(1)
    upper_chunk(1)
    ring3(0, y_ring, yn)
    xn = x_swap(0)
    pivot_chunk(1)
    for c in uf_moves[2]:
        c.wait_recv()
    upper_prep(2)
    pivot_chunk(2)

    place = (iota((Q, S), 1) == iota((Q, S), 0) + col * Q).astype(F32)
    piece = w_re * piv_ref[0, 1] + w_im * piv_ref[0, 0]
    placed = jnp.dot(piece, place, precision=lax.Precision.HIGHEST, preferred_element_type=F32)
    for g in range(32):
        at = (g % 2, (g // 4) % 4, ((g // 2) % 2) * 2 + g // 16)
        mine = (row == g // 8).astype(F32)
        pvb[at[0], at[1], at[2]] = (
            pvs[g * 8 : g * 8 + 8, :] + mine * placed[(g % 8) * 8 : (g % 8) * 8 + 8, :]
        )
    p1 = send(pvb.at[1 - core], pc, d_core)
    upper_chunk(2)
    for g in range(32):
        at = (g % 2, (g // 4) % 4, ((g // 2) % 2) * 2 + g // 16)
        cb[at[0], at[1], at[2]] = -y[g * 8 : g * 8 + 8, :]
    to_core = send(cb.at[1 - core], rc, d_core)
    ring3(1, z_ring, zf)
    yf = ring1(1, y_ring)
    p1.wait_recv()
    pvb[core] += pc[...]

    def in_plane(n, other):
        zz, xx = (z + n // 4) % 4, (x + n) % 4
        cc = (core + other) % 2
        return zz, xx, ((xx % 2) * 4 + zz, (xx // 2) * 2 + cc, col)

    p2 = []
    for n in range(1, 16):
        zz, xx, dev = in_plane(n, 0)
        p2.append(send(pvb.at[core, zz, xx], pz.at[n - 1], dev))
    x_add(0, xn)
    to_core.wait_recv()

    @pl.loop(0, 4)
    def _(b):
        cb[core, b] += rc[b]

    f1p = send(cb.at[core, z2, pl.ds(0, 2)], ru1.at[0], d_zp)
    f1m = send(cb.at[core, z2, pl.ds(2, 2)], ru1.at[1], d_zm)
    yf = ring2(1, y_ring, yf)
    for g in range(32):
        k = (g % 2) * 16 + ((g // 4) % 4) * 4 + ((g // 2) % 2) * 2 + g // 16
        bsp[k * 8 : k * 8 + 8, :] = bs_ref[g * 8 : g * 8 + 8, :]
    for c in p2:
        c.wait_recv()
    pb[col] = pvb[core, z, x] + jnp.sum(pz[...], 0)
    p4 = [send(pb.at[col], pb.at[col], at_y((col + d) % 4)) for d in range(1, 4)]
    ring3(1, y_ring, yf)
    xf = x_swap(1)
    f1p.wait_recv()
    cb[core, zp, 0:2] += ru1[0]
    f2p = send(cb.at[core, zp], ru2.at[0], d_zp)
    f1m.wait_recv()
    cb[core, zm, 2:4] += ru1[1]
    f2m = send(cb.at[core, zm], ru2.at[1], d_zm)
    for c in p4:
        c.wait_recv()
    pfull[core, z, x] = pb[0] + pb[1] + pb[2] + pb[3]
    p5 = []
    for n in range(1, 32):
        zz, xx, dev = in_plane(n // 2, n % 2)
        p5.append(send(pfull.at[core, z, x], pfull.at[core, z, x], dev))
    x_add(1, xf)
    exchange()
    f2p.wait_recv()
    f2m.wait_recv()
    cb[core, z] += ru2[0] + ru2[1]
    rest = T - LEFT
    h1p = send(cb.at[core, z, x2, :, pl.ds(0, LEFT)], rv1.at[0], d_xp)
    h1m = send(cb.at[core, z, x2, :, pl.ds(LEFT, rest)], rv1.at[1, :, pl.ds(0, rest)], d_xm)
    h1p.wait_recv()
    cb[core, z, xp, :, :LEFT] += rv1[0]
    h2p = send(cb.at[core, z, xp], rv2.at[0], d_xp)
    h1m.wait_recv()
    cb[core, z, xm, :, LEFT:] += rv1[1, :, :rest]
    h2m = send(cb.at[core, z, xm], rv2.at[1], d_xm)
    for c in p5:
        c.wait_recv()
    pivot = pfull[...].reshape(S, S)
    charge = jnp.sum(bsp[...] * three(pivot, bs_ref[...]), 0, keepdims=True)

    pltpu.make_async_copy(got.at[pl.ds(0, DEV - 1)], got.at[pl.ds(0, DEV - 1)], arecv.at[0]).wait()
    received = got[...].reshape(8 * DEV, 128)
    both = jnp.concatenate([bs_ref[0:128, :], bs_ref[128:256, :]], 1)
    projected = three(received, both)
    first = (iota((8 * DEV, 128), 0) // 4) % 2 == 0
    projected = jnp.where(first, projected[:, :128], projected[:, 128:])
    charge = charge + jnp.sum(ba8[...] * projected, 0, keepdims=True)
    h2p.wait_recv()
    h2m.wait_recv()
    out_ref[:, :T] = cb[core, z, x] + rv2[0] + rv2[1]
    out_ref[:, T:] = jnp.broadcast_to(charge, (8, 128))
    pltpu.make_async_copy(pk.at[pl.ds(0, DEV - 1)], pk.at[pl.ds(0, DEV - 1)], asend.at[0]).wait()
    for c in started:
        c.wait_send()


N_COPIES = 112


def fused(weights, tile, lower, upper, pivot, owners, basis_super, basis_ancestor):
    vmem = pl.BlockSpec(memory_space=pltpu.VMEM)
    hbm = pl.BlockSpec(memory_space=pl.ANY)
    return pl.pallas_call(
        kernel,
        out_shape=jax.ShapeDtypeStruct((8, T + 128), F32),
        in_specs=[pl.BlockSpec(memory_space=pltpu.SMEM), hbm, hbm, hbm, vmem, vmem, vmem, hbm],
        out_specs=vmem,
        scratch_shapes=[
            pltpu.VMEM((2, T, T), F32),
            pltpu.VMEM((2, T, T), BF16),
            pltpu.VMEM((2, T, T), BF16),
            pltpu.VMEM((4, 2, Q, T), F32),
            pltpu.VMEM((4, 2, Q, T), F32),
            pltpu.VMEM((2, Q, T), F32),
            pltpu.VMEM((4, S, T), BF16),
            pltpu.VMEM((4, S, T), BF16),
            pltpu.VMEM((2, S, T), BF16),
            pltpu.VMEM((2, S, T), BF16),
            pltpu.VMEM((2, T, 128), F32),
            pltpu.VMEM((2, T, 128), F32),
            pltpu.VMEM((T, S), BF16),
            pltpu.VMEM((T, S), BF16),
            pltpu.VMEM((T, S), BF16),
            pltpu.VMEM((T, S), BF16),
            pltpu.VMEM((S, T), F32),
            pltpu.VMEM((2, T, 128), F32),
            pltpu.VMEM((2, BLK, 128), F32),
            pltpu.VMEM((2, 2, BLK, 128), F32),
            pltpu.VMEM((2, SUB, 128), F32),
            pltpu.VMEM((2, 2, SUB, 128), F32),
            pltpu.VMEM((2, SUB, 128), F32),
            pltpu.VMEM((2, SUB, 128), F32),
            pltpu.VMEM((2, 4, 4, 8, T), F32),
            pltpu.VMEM((4, 4, 8, T), F32),
            pltpu.VMEM((2, 2, 8, T), F32),
            pltpu.VMEM((2, 4, 8, T), F32),
            pltpu.VMEM((2, 8, LEFT), F32),
            pltpu.VMEM((2, 8, T), F32),
            pltpu.VMEM((2, 4, 4, 8, S), F32),
            pltpu.VMEM((4, 4, 8, S), F32),
            pltpu.VMEM((15, 8, S), F32),
            pltpu.VMEM((4, 8, S), F32),
            pltpu.VMEM((2, 4, 4, 8, S), F32),
            pltpu.VMEM((S, 128), F32),
            pltpu.VMEM((4608, 128), F32),
            pltpu.VMEM((8 * DEV, 128), F32),
            pltpu.VMEM((8 * DEV, 2 * SUB), BF16),
            pltpu.VMEM((DEV, 8, 128), F32),
            pltpu.VMEM((DEV, 8, 128), F32),
            pltpu.VMEM((BAT, TOPK, WIDE), jnp.int32),
            pltpu.VMEM((S, S), F32),
            pltpu.VMEM((T, S), BF16),
            pltpu.VMEM((T, S), BF16),
            pltpu.VMEM((2, S, S), BF16),
            pltpu.SemaphoreType.DMA((N_COPIES,)),
            pltpu.SemaphoreType.DMA((N_COPIES,)),
            pltpu.SemaphoreType.DMA((7,)),
            pltpu.SemaphoreType.DMA((1,)),
            pltpu.SemaphoreType.DMA((1,)),
        ],
        compiler_params=pltpu.CompilerParams(
            collective_id=0, has_side_effects=True, vmem_limit_bytes=63 << 20
        ),
    )(weights, tile, lower, upper, pivot, owners, basis_super, basis_ancestor)


def body(
    inverse_tile, lower_factor, upper_factor, pivot_inverse, pole_weights, block_owners,
    basis_ancestor, basis_super,
):
    out = fused(
        pole_weights, inverse_tile, lower_factor, upper_factor, pivot_inverse, block_owners.T,
        basis_super, basis_ancestor,
    )
    return (out[:, :T], out[0, T:])


def solution(mesh):
    placed = (
        P("pole", None, "row", "col"),
        P("pole", None, "row", "col"),
        P("pole", None, "col", "row"),
        P("pole", None, "row", "col"),
        P("pole", None),
        P(),
        P(None, ("pole", "row", "col")),
        P(None, ("pole", "row", "col")),
    )
    return jax.shard_map(
        body,
        mesh=mesh,
        in_specs=placed,
        out_specs=(P(("pole", "row"), "col"), P(("pole", "row", "col"))),
        check_vma=False,
    )
```

```python
import jax
import jax.numpy as jnp
from jax import lax
from jax.experimental import pallas as pl
from jax.experimental.pallas import tpu as pltpu
from jax.sharding import PartitionSpec as P

MESH = pl.DeviceIdType.MESH
F32 = jnp.float32
BF16 = jnp.bfloat16
T = 1152
S = 256
Q = 64
NB = 18
TOPK = 6
BAT = 8
WIDE = 288
DEV = 128
CHUNKS = ((0, 512), (512, 512), (1024, 128))
BLK = 288
SUB = 72
TAIL = 1024


def nt(a, b):
    return lax.dot_general(a, b, (((1,), (1,)), ((), ())), preferred_element_type=F32)


def nn(a, b):
    return jnp.dot(a, b, preferred_element_type=F32)


def split(v):
    hi = v.astype(BF16)
    return hi, (v - hi.astype(F32)).astype(BF16)


def tn(a, b):
    return lax.dot_general(a, b, (((0,), (0,)), ((), ())), preferred_element_type=F32)


def iota(shape, dim):
    return lax.broadcasted_iota(jnp.int32, shape, dim)


def rows_of(start, size):
    return pl.ds(pl.multiple_of(start, 8), size)


def kernel(
    w_ref, a_hbm, l_hbm, u_hbm, piv_ref, own_ref, bs_ref, ba_hbm,
    out_ref,
    a32, ah, al, lf, uf, bl, br, uph, upl, xr, xi, xih, xil, xrh, xrl, y, lt,
    rz1, rz2, ry, rx, ld, cb, rc, ru1, ru2, rv,
    pvb, pc, pz, pb, pfull, bsp, ba, ba4, sel, pk, got, own_s, pvs, ath, atl, bt,
    sends, recvs, locs, asend, arecv,
):
    pole, row, col = lax.axis_index("pole"), lax.axis_index("row"), lax.axis_index("col")
    x_lo, z = pole // 4, pole % 4
    x_hi, core = row // 2, row % 2
    x = x_hi * 2 + x_lo
    me = (pole * 4 + row) * 4 + col
    group = row * 32 + z * 8 + col * 2 + x_lo

    def at_x(v):
        return ((v % 2) * 4 + z, (v // 2) * 2 + core, col)

    def at_y(v):
        return (pole, row, v)

    def at_z(v):
        return (x_lo * 4 + v, row, col)

    def row_x(v):
        return (v // 2) * 2 + core

    xp, xm, x2 = (x + 1) % 4, (x + 3) % 4, (x + 2) % 4
    yp, ym, y2 = (col + 1) % 4, (col + 3) % 4, (col + 2) % 4
    zp, zm, z2 = (z + 1) % 4, (z + 3) % 4, (z + 2) % 4
    d_core = (pole, x_hi * 2 + 1 - core, col)
    d_xp, d_xm = at_x(xp), at_x(xm)
    d_yp, d_ym = at_y(yp), at_y(ym)
    d_zp, d_zm = at_z(zp), at_z(zm)
    d_xn = at_x(x_hi * 2 + 1 - x_lo)
    started = []

    def send(src, dst, dev):
        n = len(started)
        c = pltpu.make_async_remote_copy(
            src_ref=src, dst_ref=dst, send_sem=sends.at[n], recv_sem=recvs.at[n],
            device_id=dev, device_id_type=MESH,
        )
        c.start()
        started.append(c)
        return c

    local_a = []
    for b in range(4):
        rs = slice(b * BLK, (b + 1) * BLK)
        c = pltpu.make_async_copy(a_hbm.at[0, :, rs, :], a32.at[:, rs, :], locs.at[b])
        local_a.append(c)
    local_l = pltpu.make_async_copy(l_hbm.at[0], lf.at[row], locs.at[4])
    local_u = pltpu.make_async_copy(u_hbm.at[0], uf.at[col], locs.at[5])
    local_ba = pltpu.make_async_copy(ba_hbm, ba, locs.at[6])
    local_l.start()
    for c in local_a:
        c.start()

    def split_a(b):
        local_a[b].wait()

        @pl.loop(0, BLK // 16)
        def _(i):
            rs = pl.ds(pl.multiple_of(b * BLK + i * 16, 16), 16)
            for part in range(2):
                hi, low = split(a32[part, rs, :])
                ah[part, rs, :] = hi
                al[part, rs, :] = low
                ath[rs, part * 128 : part * 128 + 128] = hi[:, TAIL:]
                atl[rs, part * 128 : part * 128 + 128] = low[:, TAIL:]

    barrier = pltpu.get_barrier_semaphore()
    greet = (d_core, d_xp, d_xm, at_x(x2), d_yp, d_ym, d_zp, d_zm)
    for dev in greet:
        pl.semaphore_signal(barrier, inc=1, device_id=dev, device_id_type=MESH)
    split_a(0)
    pl.semaphore_wait(barrier, len(greet))

    def lanes(k):
        return pl.ds(CHUNKS[k][0], CHUNKS[k][1])

    def l_own(k):
        return send(l_hbm.at[0, :, :, lanes(k)], lf.at[row, :, :, lanes(k)], at_x(x2))

    far = (1 - x_hi) * 2 + core

    def l_share(k, own):
        own.wait_recv()
        return send(lf.at[far, :, :, lanes(k)], lf.at[far, :, :, lanes(k)], d_core)

    def u_own(k):
        return (
            send(u_hbm.at[0, :, :, lanes(k)], uf.at[col, :, :, lanes(k)], d_yp),
            send(u_hbm.at[0, :, :, lanes(k)], uf.at[col, :, :, lanes(k)], d_ym),
        )

    def u_forward(k, own):
        own[0].wait_recv()
        p = send(uf.at[ym, 0, :, lanes(k)], uf.at[ym, 0, :, lanes(k)], d_yp)
        own[1].wait_recv()
        m = send(uf.at[yp, 1, :, lanes(k)], uf.at[yp, 1, :, lanes(k)], d_ym)
        return p, m

    l_near, lo, uo = [], [], []
    for k in range(3):
        l_near.append(send(l_hbm.at[0, :, :, lanes(k)], lf.at[row, :, :, lanes(k)], d_core))
        lo.append(l_own(k))
        uo.append(u_own(k))
    local_ba.start()
    local_u.start()

    w_re, w_im = w_ref[0, 0], w_ref[0, 1]

    def build(dst, slot, q, lane):
        re, im = lf[slot, 0, :, lane], lf[slot, 1, :, lane]
        a, b = pl.ds(q * Q, Q), pl.ds(2 * Q + q * Q, Q)
        rh, rl = split(re)
        ih, il = split(im)
        if lane.start == TAIL:
            one, two = pl.ds(0, 128), pl.ds(128, 128)
            bt[0, a, one], bt[1, a, one] = rh, rl
            bt[0, b, one], bt[1, b, one] = ih, il
            bt[0, a, two], bt[1, a, two] = -ih, -il
            bt[0, b, two], bt[1, b, two] = rh, rl
            return
        dst[0, a, lane], dst[1, a, lane] = rh, rl
        dst[0, b, lane], dst[1, b, lane] = ih, il
        dst[2, a, lane], dst[3, a, lane] = -ih, -il
        dst[2, b, lane], dst[3, b, lane] = rh, rl

    def product(rs, lane, b):
        acc = nt(ah[0, rs, lane], b[0, :, lane])
        acc = acc + nt(ah[0, rs, lane], b[1, :, lane])
        acc = acc + nt(al[0, rs, lane], b[0, :, lane])
        acc = acc + nt(ah[1, rs, lane], b[2, :, lane])
        acc = acc + nt(ah[1, rs, lane], b[3, :, lane])
        acc = acc + nt(al[1, rs, lane], b[2, :, lane])
        return acc

    halves = (x_hi, 1 - x_hi)

    def lower_term(n):
        h = halves[n]

        @pl.loop(0, 4)
        def _(b):
            rs = pl.ds(pl.multiple_of(b * BLK, 16), BLK)
            lt[h, rs, :] = -(w_re * xi[h, rs, :] + w_im * xr[h, rs, :])

    def z_at(b):
        return b * BLK

    def y_at(b):
        return z * BLK + b * SUB

    z_ring = (z_at, BLK, 144, (zp, zm, z2, z), (d_zp, d_zm), rz1, rz2)

    def y_send(n):
        h = halves[n]
        return [
            send(lt.at[h, rows_of(y_at((col + d) % 4), SUB), :], ry.at[n, d - 1], at_y((col + d) % 4))
            for d in range(1, 4)
        ]

    def y_sum(n, before):
        for c in before:
            c.wait_recv()
        lt[halves[n], rows_of(y_at(col), SUB), :] += ry[n, 0] + ry[n, 1] + ry[n, 2]

    def ring1(n, ring):
        at, size, first, (p, m, two, own), (dp, dm), r1, r2 = ring
        h = halves[n]
        return (
            send(lt.at[h, rows_of(at(two), first), :], r1.at[n, pl.ds(0, first), :], dp),
            send(
                lt.at[h, rows_of(at(two) + first, size - first), :],
                r1.at[n, pl.ds(first, size - first), :], dm,
            ),
        )

    def ring2(n, ring, before):
        at, size, first, (p, m, two, own), (dp, dm), r1, r2 = ring
        h = halves[n]
        before[0].wait_recv()
        lt[h, rows_of(at(p), first), :] += r1[n, 0:first]
        a = send(lt.at[h, rows_of(at(p), size), :], r2.at[n, 0], dp)
        before[1].wait_recv()
        lt[h, rows_of(at(m) + first, size - first), :] += r1[n, first:size]
        return a, send(lt.at[h, rows_of(at(m), size), :], r2.at[n, 1], dm)

    def ring3(n, ring, before):
        at, size, first, (p, m, two, own), (dp, dm), r1, r2 = ring
        before[0].wait_recv()
        before[1].wait_recv()
        lt[halves[n], rows_of(at(own), size), :] += r2[n, 0] + r2[n, 1]

    def x_swap(n):
        return send(lt.at[halves[n], rows_of(y_at(col), SUB), :], rx.at[n], d_xn)

    def x_add(n, before):
        before.wait_recv()
        ld[halves[n]] = lt[halves[n], rows_of(y_at(col), SUB), :] + rx[n]

    def upper_prep(k):
        lane = lanes(k)
        for q in range(4):
            re, im = uf[q, 0, :, lane], uf[q, 1, :, lane]
            rs = pl.ds(q * Q, Q)
            for part, v in ((0, w_re * re - w_im * im), (1, w_re * im + w_im * re)):
                hi, low = split(v)
                uph[part, rs, lane] = hi
                upl[part, rs, lane] = low

    def upper_chunk(k):
        lane = lanes(k)
        acc = nn(uph[0, :, lane], ah[1, lane, :])
        acc = acc + nn(uph[0, :, lane], al[1, lane, :])
        acc = acc + nn(upl[0, :, lane], ah[1, lane, :])
        acc = acc + nn(uph[1, :, lane], ah[0, lane, :])
        acc = acc + nn(uph[1, :, lane], al[0, lane, :])
        acc = acc + nn(upl[1, :, lane], ah[0, lane, :])
        if k == 0:
            y[...] = acc
        else:
            y[...] += acc

    def chunk(n, k, blocks=(0, 4)):
        dst, h = ((bl, br)[n], halves[n])
        if blocks[0] == 0:
            for q in range(2):
                build(dst, h * 2 + q, q, lanes(k))

        @pl.loop(*blocks)
        def _(b):
            rs = pl.ds(pl.multiple_of(b * BLK, 16), BLK)
            if k == 2:
                acc = nt(ath[rs, :], bt[0]) + nt(ath[rs, :], bt[1]) + nt(atl[rs, :], bt[0])
            else:
                acc = product(rs, lanes(k), dst)
            if k == 0:
                xr[h, rs, :] = acc[:, :128]
                xi[h, rs, :] = acc[:, 128:]
            else:
                xr[h, rs, :] += acc[:, :128]
                xi[h, rs, :] += acc[:, 128:]

    def pivot_chunk(k):
        lane = lanes(k)
        acc = nn(uph[0, :, lane], xih[lane, :])
        acc = acc + nn(uph[0, :, lane], xil[lane, :])
        acc = acc + nn(upl[0, :, lane], xih[lane, :])
        acc = acc + nn(uph[1, :, lane], xrh[lane, :])
        acc = acc + nn(uph[1, :, lane], xrl[lane, :])
        acc = acc + nn(upl[1, :, lane], xrh[lane, :])
        if k == 0:
            pvs[...] = acc
        else:
            pvs[...] += acc

    def choose_rows():
        for b in range(BAT):
            own_s[b] = own_ref[:, b * WIDE : (b + 1) * WIDE]
        mine = own_s[group // 16].astype(F32).astype(BF16)
        here = nn(
            mine,
            (iota((WIDE, NB), 0) == (group % 16) * NB + iota((WIDE, NB), 1)).astype(F32).astype(BF16),
        )
        owner = iota((2 * DEV, NB), 0)
        named = jnp.zeros((2 * DEV, NB), F32)
        for t in range(TOPK):
            hit = here[t : t + 1, :] == (owner // 2).astype(F32)
            named = jnp.maximum(named, hit.astype(F32))
        earlier = (iota((NB, NB), 0) < iota((NB, NB), 1)).astype(F32).astype(BF16)
        rank = nn(named.astype(BF16), earlier)
        chosen = named * (rank == (owner % 2).astype(F32)).astype(F32)
        spot = iota((NB, SUB), 1)
        spread = (
            (spot // 36 == x_lo) & ((spot % 36) // 2 == iota((NB, SUB), 0))
        ).astype(F32)
        wide = nn(chosen.astype(BF16), spread.astype(BF16))
        out = iota((4 * DEV, 2 * DEV), 0)
        repeat = (iota((4 * DEV, 2 * DEV), 1) == out // 2).astype(F32)
        full = nn(repeat.astype(BF16), wide.astype(BF16))
        keep = iota((4 * DEV, SUB), 0) % 2 == iota((4 * DEV, SUB), 1) % 2
        sel[...] = jnp.where(keep, full, 0.0).astype(BF16)

    def choose_ancestors(start, stop):
        if start == 0:
            local_ba.wait()
        block = iota((WIDE, WIDE), 0), iota((WIDE, WIDE), 1)
        earlier = ((block[0] // NB == block[1] // NB) & (block[0] < block[1])).astype(F32)
        earlier = earlier.astype(BF16)
        slot = iota((4 * 16, WIDE), 0)
        wanted = slot - slot % 2

        @pl.loop(start, stop)
        def _(b):
            owners = own_s[b]
            mine = jnp.max((owners == me).astype(F32), 0, keepdims=True)
            rank = nn(jnp.broadcast_to(mine, (8, WIDE)).astype(BF16), earlier)[0:1, :]
            base = (iota((1, WIDE), 1) // NB * 4).astype(F32)
            key = jnp.where(mine > 0, base + 2 * rank, -8.0)
            hit = key == wanted.astype(F32)
            acc = jnp.zeros((4 * 16, 128), F32)
            for parity in range(2):
                one = (hit & (slot % 2 == parity)).astype(F32).astype(BF16)
                v = ba[pl.ds(b * 2 * WIDE + parity, WIDE, stride=2), :]
                hi, low = split(v)
                acc = acc + nn(one, hi) + nn(one, low)
            ba4[rows_of(b * 64, 64), :] = acc

    def exchange(n):
        h = halves[n]
        v = ld[h]
        hi, low = split(v)
        rest = (v - hi.astype(F32) - low.astype(F32)).astype(BF16)
        packed = nn(sel[...], hi) + nn(sel[...], low) + nn(sel[...], rest)
        pk[n] = packed.reshape(DEV, 4, 128)
        got[h, group] = pk[n, me]
        for i in range(1, DEV):
            p, r, c = (pole + i // 16) % 8, (row + i // 4) % 4, (col + i) % 4
            pltpu.make_async_remote_copy(
                src_ref=pk.at[n, (p * 4 + r) * 4 + c], dst_ref=got.at[h, group],
                send_sem=asend.at[n], recv_sem=arecv.at[h],
                device_id=(p, r, c), device_id_type=MESH,
            ).start()

    def three(a, b):
        ahi, alo = split(a)
        bhi, blo = split(b)
        return nn(ahi, bhi) + nn(ahi, blo) + nn(alo, bhi)

    for b in range(1, 4):
        split_a(b)
    local_l.wait()
    l_near[0].wait_recv()
    chunk(0, 0)
    l_near[1].wait_recv()
    chunk(0, 1)
    l_near[2].wait_recv()
    chunk(0, 2)
    ls = [l_share(0, lo[0])]
    lower_term(0)
    zn = ring1(0, z_ring)
    choose_rows()
    uf_moves = [u_forward(0, uo[0])]
    choose_ancestors(0, 4)
    ls[0].wait_recv()
    chunk(1, 0, (0, 2))
    zn = ring2(0, z_ring, zn)
    chunk(1, 0, (2, 4))
    uf_moves.append(u_forward(1, uo[1]))
    ls.append(l_share(1, lo[1]))
    choose_ancestors(4, 8)
    ls.append(l_share(2, lo[2]))
    uf_moves.append(u_forward(2, uo[2]))
    local_u.wait()
    ls[1].wait_recv()
    chunk(1, 1, (0, 2))
    ring3(0, z_ring, zn)
    yn = y_send(0)
    chunk(1, 1, (2, 4))
    ls[2].wait_recv()
    chunk(1, 2)
    lower_term(1)
    zf = ring1(1, z_ring)
    for h in range(2):
        hs = pl.ds(h * 128, 128)
        hi, low = split(xi[h])
        xih[:, hs], xil[:, hs] = hi, low
        hi, low = split(xr[h])
        xrh[:, hs], xrl[:, hs] = hi, low
    for c in uf_moves[0]:
        c.wait_recv()
    upper_prep(0)
    upper_chunk(0)
    y_sum(0, yn)
    xn = x_swap(0)
    pivot_chunk(0)
    zf = ring2(1, z_ring, zf)
    for c in uf_moves[1]:
        c.wait_recv()
    upper_prep(1)
    upper_chunk(1)
    x_add(0, xn)
    exchange(0)
    pivot_chunk(1)
    for c in uf_moves[2]:
        c.wait_recv()
    upper_prep(2)
    pivot_chunk(2)

    place = (iota((Q, S), 1) == iota((Q, S), 0) + col * Q).astype(F32)
    piece = w_re * piv_ref[0, 1] + w_im * piv_ref[0, 0]
    placed = jnp.dot(piece, place, precision=lax.Precision.HIGHEST, preferred_element_type=F32)
    for g in range(32):
        at = (g % 2, (g // 4) % 4, ((g // 2) % 2) * 2 + g // 16)
        mine = (row == g // 8).astype(F32)
        pvb[at[0], at[1], at[2]] = (
            pvs[g * 8 : g * 8 + 8, :] + mine * placed[(g % 8) * 8 : (g % 8) * 8 + 8, :]
        )
    p1 = send(pvb.at[1 - core], pc, d_core)
    ring3(1, z_ring, zf)
    yf = y_send(1)
    upper_chunk(2)
    for g in range(32):
        at = (g % 2, (g // 4) % 4, ((g // 2) % 2) * 2 + g // 16)
        cb[at[0], at[1], at[2]] = -y[g * 8 : g * 8 + 8, :]
    to_core = send(cb.at[1 - core], rc, d_core)
    p1.wait_recv()
    pvb[core] += pc[...]

    def in_plane(n):
        zz, xx = (z + n // 4) % 4, (x + n) % 4
        return zz, xx, ((xx % 2) * 4 + zz, (xx // 2) * 2 + core, col)

    p2 = []
    for n in range(1, 16):
        zz, xx, dev = in_plane(n)
        p2.append(send(pvb.at[core, zz, xx], pz.at[n - 1], dev))
    to_core.wait_recv()

    @pl.loop(0, 4)
    def _(b):
        cb[core, b] += rc[b]

    f1p = send(cb.at[core, z2, pl.ds(0, 2)], ru1.at[0], d_zp)
    f1m = send(cb.at[core, z2, pl.ds(2, 2)], ru1.at[1], d_zm)
    y_sum(1, yf)
    xf = x_swap(1)
    for g in range(32):
        k = (g % 2) * 16 + ((g // 4) % 4) * 4 + ((g // 2) % 2) * 2 + g // 16
        bsp[k * 8 : k * 8 + 8, :] = bs_ref[g * 8 : g * 8 + 8, :]
    for c in p2:
        c.wait_recv()
    pb[col] = pvb[core, z, x] + jnp.sum(pz[...], 0)
    p4 = [send(pb.at[col], pb.at[col], at_y((col + d) % 4)) for d in range(1, 4)]
    f1p.wait_recv()
    cb[core, zp, 0:2] += ru1[0]
    f2p = send(cb.at[core, zp], ru2.at[0], d_zp)
    f1m.wait_recv()
    cb[core, zm, 2:4] += ru1[1]
    f2m = send(cb.at[core, zm], ru2.at[1], d_zm)
    for c in p4:
        c.wait_recv()
    pfull[core, z, x] = pb[0] + pb[1] + pb[2] + pb[3]
    p5 = []
    for n in range(1, 16):
        zz, xx, dev = in_plane(n)
        p5.append(send(pfull.at[core, z, x], pfull.at[core, z, x], dev))
    x_add(1, xf)
    exchange(1)
    f2p.wait_recv()
    f2m.wait_recv()
    cb[core, z] += ru2[0] + ru2[1]
    h1 = [
        send(cb.at[core, z, (x + d) % 4], rv.at[d - 1], at_x((x + d) % 4)) for d in range(1, 4)
    ]
    for c in p5:
        c.wait_recv()
    p6 = send(pfull.at[core], pfull.at[core], d_core)
    for c in h1:
        c.wait_recv()
    out_ref[:, :T] = cb[core, z, x] + rv[0] + rv[1] + rv[2]
    p6.wait_recv()
    pivot = pfull[...].reshape(S, S)
    charge = jnp.sum(bsp[...] * three(pivot, bs_ref[...]), 0, keepdims=True)
    others = pl.ds(0, DEV - 1)
    for h in range(2):
        pltpu.make_async_copy(got.at[h, others], got.at[h, others], arecv.at[h]).wait()
    received = jnp.concatenate([got[h].reshape(4 * DEV, 128) for h in range(2)], 1)
    projected = three(received, bs_ref[...])
    charge = charge + jnp.sum(ba4[...] * projected, 0, keepdims=True)
    out_ref[:, T:] = jnp.broadcast_to(charge, (8, 128))
    for n in range(2):
        pltpu.make_async_copy(pk.at[n, others], pk.at[n, others], asend.at[n]).wait()
    for c in started:
        c.wait_send()


N_COPIES = 112


def hand_out(both_ref, upper_ref, charge_ref):
    upper_ref[...] = both_ref[:, :T]
    charge_ref[...] = both_ref[0:1, T:]


def fused(weights, tile, lower, upper, pivot, owners, basis_super, basis_ancestor):
    vmem = pl.BlockSpec(memory_space=pltpu.VMEM)
    hbm = pl.BlockSpec(memory_space=pl.ANY)
    return pl.pallas_call(
        kernel,
        out_shape=jax.ShapeDtypeStruct((8, T + 128), F32),
        in_specs=[pl.BlockSpec(memory_space=pltpu.SMEM), hbm, hbm, hbm, vmem, vmem, vmem, hbm],
        out_specs=vmem,
        scratch_shapes=[
            pltpu.VMEM((2, T, T), F32),
            pltpu.VMEM((2, T, T), BF16),
            pltpu.VMEM((2, T, T), BF16),
            pltpu.VMEM((4, 2, Q, T), F32),
            pltpu.VMEM((4, 2, Q, T), F32),
            pltpu.VMEM((4, S, T), BF16),
            pltpu.VMEM((4, S, T), BF16),
            pltpu.VMEM((2, S, T), BF16),
            pltpu.VMEM((2, S, T), BF16),
            pltpu.VMEM((2, T, 128), F32),
            pltpu.VMEM((2, T, 128), F32),
            pltpu.VMEM((T, S), BF16),
            pltpu.VMEM((T, S), BF16),
            pltpu.VMEM((T, S), BF16),
            pltpu.VMEM((T, S), BF16),
            pltpu.VMEM((S, T), F32),
            pltpu.VMEM((2, T, 128), F32),
            pltpu.VMEM((2, BLK, 128), F32),
            pltpu.VMEM((2, 2, BLK, 128), F32),
            pltpu.VMEM((2, 3, SUB, 128), F32),
            pltpu.VMEM((2, SUB, 128), F32),
            pltpu.VMEM((2, SUB, 128), F32),
            pltpu.VMEM((2, 4, 4, 8, T), F32),
            pltpu.VMEM((4, 4, 8, T), F32),
            pltpu.VMEM((2, 2, 8, T), F32),
            pltpu.VMEM((2, 4, 8, T), F32),
            pltpu.VMEM((3, 8, T), F32),
            pltpu.VMEM((2, 4, 4, 8, S), F32),
            pltpu.VMEM((4, 4, 8, S), F32),
            pltpu.VMEM((15, 8, S), F32),
            pltpu.VMEM((4, 8, S), F32),
            pltpu.VMEM((2, 4, 4, 8, S), F32),
            pltpu.VMEM((S, 128), F32),
            pltpu.VMEM((4608, 128), F32),
            pltpu.VMEM((4 * DEV, 128), F32),
            pltpu.VMEM((4 * DEV, SUB), BF16),
            pltpu.VMEM((2, DEV, 4, 128), F32),
            pltpu.VMEM((2, DEV, 4, 128), F32),
            pltpu.VMEM((BAT, TOPK, WIDE), jnp.int32),
            pltpu.VMEM((S, S), F32),
            pltpu.VMEM((T, S), BF16),
            pltpu.VMEM((T, S), BF16),
            pltpu.VMEM((2, S, S), BF16),
            pltpu.SemaphoreType.DMA((N_COPIES,)),
            pltpu.SemaphoreType.DMA((N_COPIES,)),
            pltpu.SemaphoreType.DMA((7,)),
            pltpu.SemaphoreType.DMA((2,)),
            pltpu.SemaphoreType.DMA((2,)),
        ],
        compiler_params=pltpu.CompilerParams(
            collective_id=0, has_side_effects=True, vmem_limit_bytes=63 << 20
        ),
    )(weights, tile, lower, upper, pivot, owners, basis_super, basis_ancestor)


def body(
    inverse_tile, lower_factor, upper_factor, pivot_inverse, pole_weights, block_owners,
    basis_ancestor, basis_super,
):
    out = fused(
        pole_weights, inverse_tile, lower_factor, upper_factor, pivot_inverse, block_owners.T,
        basis_super, basis_ancestor,
    )
    upper_density, charge = pl.pallas_call(
        hand_out,
        out_shape=(jax.ShapeDtypeStruct((8, T), F32), jax.ShapeDtypeStruct((1, 128), F32)),
    )(out)
    return (upper_density, charge.reshape(128))


def solution(mesh):
    placed = (
        P("pole", None, "row", "col"),
        P("pole", None, "row", "col"),
        P("pole", None, "col", "row"),
        P("pole", None, "row", "col"),
        P("pole", None),
        P(),
        P(None, ("pole", "row", "col")),
        P(None, ("pole", "row", "col")),
    )
    return jax.shard_map(
        body,
        mesh=mesh,
        in_specs=placed,
        out_specs=(P(("pole", "row"), "col"), P(("pole", "row", "col"))),
        check_vma=False,
    )
```

```python
import jax
import jax.numpy as jnp
from jax import lax
from jax.experimental import pallas as pl
from jax.experimental.pallas import tpu as pltpu
from jax.sharding import PartitionSpec as P

MESH = pl.DeviceIdType.MESH
F32 = jnp.float32
BF16 = jnp.bfloat16
T = 1152
S = 256
Q = 64
NB = 18
TOPK = 6
BAT = 8
WIDE = 288
DEV = 128
CHUNKS = ((0, 512), (512, 512), (1024, 128))
BLK = 288
SUB = 72
TAIL = 1024
LEFT = 640


def nt(a, b):
    return lax.dot_general(a, b, (((1,), (1,)), ((), ())), preferred_element_type=F32)


def nn(a, b):
    return jnp.dot(a, b, preferred_element_type=F32)


def split(v):
    hi = v.astype(BF16)
    return hi, (v - hi.astype(F32)).astype(BF16)


def tn(a, b):
    return lax.dot_general(a, b, (((0,), (0,)), ((), ())), preferred_element_type=F32)


def iota(shape, dim):
    return lax.broadcasted_iota(jnp.int32, shape, dim)


def rows_of(start, size):
    return pl.ds(pl.multiple_of(start, 8), size)


def kernel(
    w_ref, a_hbm, l_hbm, u_hbm, piv_ref, own_ref, bs_ref, ba_hbm,
    out_ref,
    a32, ah, al, lf, uf, bl, br, uph, upl, xr, xi, xih, xil, xrh, xrl, y, lt,
    rz1, rz2, ry, rx, ld, cb, rc, ra, rb, rv,
    pvb, pc, pz, pb, pfull, bsp, ba, ba4, sel, pk, got, own_s, pvs, ath, atl, bt,
    sends, recvs, locs, asend, arecv,
):
    pole, row, col = lax.axis_index("pole"), lax.axis_index("row"), lax.axis_index("col")
    x_lo, z = pole // 4, pole % 4
    x_hi, core = row // 2, row % 2
    x = x_hi * 2 + x_lo
    me = (pole * 4 + row) * 4 + col
    group = row * 32 + z * 8 + col * 2 + x_lo

    def at_x(v):
        return ((v % 2) * 4 + z, (v // 2) * 2 + core, col)

    def at_y(v):
        return (pole, row, v)

    def at_z(v):
        return (x_lo * 4 + v, row, col)

    def row_x(v):
        return (v // 2) * 2 + core

    xp, xm, x2 = (x + 1) % 4, (x + 3) % 4, (x + 2) % 4
    yp, ym, y2 = (col + 1) % 4, (col + 3) % 4, (col + 2) % 4
    zp, zm, z2 = (z + 1) % 4, (z + 3) % 4, (z + 2) % 4
    d_core = (pole, x_hi * 2 + 1 - core, col)
    d_xp, d_xm = at_x(xp), at_x(xm)
    d_yp, d_ym = at_y(yp), at_y(ym)
    d_zp, d_zm = at_z(zp), at_z(zm)
    d_xn = at_x(x_hi * 2 + 1 - x_lo)
    started = []

    def send(src, dst, dev):
        n = len(started)
        c = pltpu.make_async_remote_copy(
            src_ref=src, dst_ref=dst, send_sem=sends.at[n], recv_sem=recvs.at[n],
            device_id=dev, device_id_type=MESH,
        )
        c.start()
        started.append(c)
        return c

    local_a = []
    for b in range(4):
        rs = slice(b * BLK, (b + 1) * BLK)
        c = pltpu.make_async_copy(a_hbm.at[0, :, rs, :], a32.at[:, rs, :], locs.at[b])
        local_a.append(c)
    local_l = pltpu.make_async_copy(l_hbm.at[0], lf.at[row], locs.at[4])
    local_u = pltpu.make_async_copy(u_hbm.at[0], uf.at[col], locs.at[5])
    local_ba = pltpu.make_async_copy(ba_hbm, ba, locs.at[6])
    local_l.start()
    for c in local_a:
        c.start()

    def split_a(b):
        local_a[b].wait()

        @pl.loop(0, BLK // 16)
        def _(i):
            rs = pl.ds(pl.multiple_of(b * BLK + i * 16, 16), 16)
            for part in range(2):
                hi, low = split(a32[part, rs, :])
                ah[part, rs, :] = hi
                al[part, rs, :] = low
                ath[rs, part * 128 : part * 128 + 128] = hi[:, TAIL:]
                atl[rs, part * 128 : part * 128 + 128] = low[:, TAIL:]

    barrier = pltpu.get_barrier_semaphore()
    greet = (d_core, d_xp, d_xm, at_x(x2), d_yp, d_ym, d_zp, d_zm)
    for dev in greet:
        pl.semaphore_signal(barrier, inc=1, device_id=dev, device_id_type=MESH)
    split_a(0)
    pl.semaphore_wait(barrier, len(greet))

    def lanes(k):
        return pl.ds(CHUNKS[k][0], CHUNKS[k][1])

    def l_own(k):
        return send(l_hbm.at[0, :, :, lanes(k)], lf.at[row, :, :, lanes(k)], at_x(x2))

    far = (1 - x_hi) * 2 + core

    def l_share(k, own):
        own.wait_recv()
        return send(lf.at[far, :, :, lanes(k)], lf.at[far, :, :, lanes(k)], d_core)

    def u_own(k):
        return (
            send(u_hbm.at[0, :, :, lanes(k)], uf.at[col, :, :, lanes(k)], d_yp),
            send(u_hbm.at[0, :, :, lanes(k)], uf.at[col, :, :, lanes(k)], d_ym),
        )

    def u_forward(k, own):
        own[0].wait_recv()
        p = send(uf.at[ym, 0, :, lanes(k)], uf.at[ym, 0, :, lanes(k)], d_yp)
        own[1].wait_recv()
        m = send(uf.at[yp, 1, :, lanes(k)], uf.at[yp, 1, :, lanes(k)], d_ym)
        return p, m

    l_near, lo, uo = [], [], []
    for k in range(3):
        l_near.append(send(l_hbm.at[0, :, :, lanes(k)], lf.at[row, :, :, lanes(k)], d_core))
        lo.append(l_own(k))
        uo.append(u_own(k))
    local_ba.start()
    local_u.start()

    w_re, w_im = w_ref[0, 0], w_ref[0, 1]

    def build(dst, slot, q, lane):
        re, im = lf[slot, 0, :, lane], lf[slot, 1, :, lane]
        a, b = pl.ds(q * Q, Q), pl.ds(2 * Q + q * Q, Q)
        rh, rl = split(re)
        ih, il = split(im)
        if lane.start == TAIL:
            one, two = pl.ds(0, 128), pl.ds(128, 128)
            bt[0, a, one], bt[1, a, one] = rh, rl
            bt[0, b, one], bt[1, b, one] = ih, il
            bt[0, a, two], bt[1, a, two] = -ih, -il
            bt[0, b, two], bt[1, b, two] = rh, rl
            return
        dst[0, a, lane], dst[1, a, lane] = rh, rl
        dst[0, b, lane], dst[1, b, lane] = ih, il
        dst[2, a, lane], dst[3, a, lane] = -ih, -il
        dst[2, b, lane], dst[3, b, lane] = rh, rl

    def product(rs, lane, b):
        acc = nt(ah[0, rs, lane], b[0, :, lane])
        acc = acc + nt(ah[0, rs, lane], b[1, :, lane])
        acc = acc + nt(al[0, rs, lane], b[0, :, lane])
        acc = acc + nt(ah[1, rs, lane], b[2, :, lane])
        acc = acc + nt(ah[1, rs, lane], b[3, :, lane])
        acc = acc + nt(al[1, rs, lane], b[2, :, lane])
        return acc

    halves = (x_hi, 1 - x_hi)

    def lower_term(n):
        h = halves[n]

        @pl.loop(0, 4)
        def _(b):
            rs = pl.ds(pl.multiple_of(b * BLK, 16), BLK)
            lt[h, rs, :] = -(w_re * xi[h, rs, :] + w_im * xr[h, rs, :])

    def z_at(b):
        return b * BLK

    def y_at(b):
        return z * BLK + b * SUB

    z_ring = (z_at, BLK, 144, (zp, zm, z2, z), (d_zp, d_zm), rz1, rz2)

    def y_send(n):
        h = halves[n]
        return [
            send(lt.at[h, rows_of(y_at((col + d) % 4), SUB), :], ry.at[n, d - 1], at_y((col + d) % 4))
            for d in range(1, 4)
        ]

    def y_sum(n, before):
        for c in before:
            c.wait_recv()
        lt[halves[n], rows_of(y_at(col), SUB), :] += ry[n, 0] + ry[n, 1] + ry[n, 2]

    def ring1(n, ring):
        at, size, first, (p, m, two, own), (dp, dm), r1, r2 = ring
        h = halves[n]
        return (
            send(lt.at[h, rows_of(at(two), first), :], r1.at[n, pl.ds(0, first), :], dp),
            send(
                lt.at[h, rows_of(at(two) + first, size - first), :],
                r1.at[n, pl.ds(first, size - first), :], dm,
            ),
        )

    def ring2(n, ring, before):
        at, size, first, (p, m, two, own), (dp, dm), r1, r2 = ring
        h = halves[n]
        before[0].wait_recv()
        lt[h, rows_of(at(p), first), :] += r1[n, 0:first]
        a = send(lt.at[h, rows_of(at(p), size), :], r2.at[n, 0], dp)
        before[1].wait_recv()
        lt[h, rows_of(at(m) + first, size - first), :] += r1[n, first:size]
        return a, send(lt.at[h, rows_of(at(m), size), :], r2.at[n, 1], dm)

    def ring3(n, ring, before):
        at, size, first, (p, m, two, own), (dp, dm), r1, r2 = ring
        before[0].wait_recv()
        before[1].wait_recv()
        lt[halves[n], rows_of(at(own), size), :] += r2[n, 0] + r2[n, 1]

    def x_swap(n):
        return send(lt.at[halves[n], rows_of(y_at(col), SUB), :], rx.at[n], d_xn)

    def x_add(n, before):
        before.wait_recv()
        ld[halves[n]] = lt[halves[n], rows_of(y_at(col), SUB), :] + rx[n]

    def upper_prep(k):
        lane = lanes(k)
        for q in range(4):
            re, im = uf[q, 0, :, lane], uf[q, 1, :, lane]
            rs = pl.ds(q * Q, Q)
            for part, v in ((0, w_re * re - w_im * im), (1, w_re * im + w_im * re)):
                hi, low = split(v)
                uph[part, rs, lane] = hi
                upl[part, rs, lane] = low

    def upper_chunk(k, parts=(0, 1)):
        lane = lanes(k)
        acc = None
        for part in parts:
            for left, right in ((uph, ah), (uph, al), (upl, ah)):
                one = nn(left[part, :, lane], right[1 - part, lane, :])
                acc = one if acc is None else acc + one
        if k == 0:
            y[...] = acc
        else:
            y[...] += acc

    def chunk(n, k, blocks=(0, 4)):
        dst, h = ((bl, br)[n], halves[n])
        if blocks[0] == 0:
            for q in range(2):
                build(dst, h * 2 + q, q, lanes(k))

        @pl.loop(*blocks)
        def _(b):
            rs = pl.ds(pl.multiple_of(b * BLK, 16), BLK)
            if k == 2:
                acc = nt(ath[rs, :], bt[0]) + nt(ath[rs, :], bt[1]) + nt(atl[rs, :], bt[0])
            else:
                acc = product(rs, lanes(k), dst)
            if k == 0:
                xr[h, rs, :] = acc[:, :128]
                xi[h, rs, :] = acc[:, 128:]
            else:
                xr[h, rs, :] += acc[:, :128]
                xi[h, rs, :] += acc[:, 128:]

    def pivot_chunk(k):
        lane = lanes(k)
        acc = nn(uph[0, :, lane], xih[lane, :])
        acc = acc + nn(uph[0, :, lane], xil[lane, :])
        acc = acc + nn(upl[0, :, lane], xih[lane, :])
        acc = acc + nn(uph[1, :, lane], xrh[lane, :])
        acc = acc + nn(uph[1, :, lane], xrl[lane, :])
        acc = acc + nn(upl[1, :, lane], xrh[lane, :])
        if k == 0:
            pvs[...] = acc
        else:
            pvs[...] += acc

    def choose_rows():
        for b in range(BAT):
            own_s[b] = own_ref[:, b * WIDE : (b + 1) * WIDE]
        mine = own_s[group // 16].astype(F32).astype(BF16)
        here = nn(
            mine,
            (iota((WIDE, NB), 0) == (group % 16) * NB + iota((WIDE, NB), 1)).astype(F32).astype(BF16),
        )
        owner = iota((2 * DEV, NB), 0)
        named = jnp.zeros((2 * DEV, NB), F32)
        for t in range(TOPK):
            hit = here[t : t + 1, :] == (owner // 2).astype(F32)
            named = jnp.maximum(named, hit.astype(F32))
        earlier = (iota((NB, NB), 0) < iota((NB, NB), 1)).astype(F32).astype(BF16)
        rank = nn(named.astype(BF16), earlier)
        chosen = named * (rank == (owner % 2).astype(F32)).astype(F32)
        spot = iota((NB, SUB), 1)
        spread = (
            (spot // 36 == x_lo) & ((spot % 36) // 2 == iota((NB, SUB), 0))
        ).astype(F32)
        wide = nn(chosen.astype(BF16), spread.astype(BF16))
        out = iota((4 * DEV, 2 * DEV), 0)
        repeat = (iota((4 * DEV, 2 * DEV), 1) == out // 2).astype(F32)
        full = nn(repeat.astype(BF16), wide.astype(BF16))
        keep = iota((4 * DEV, SUB), 0) % 2 == iota((4 * DEV, SUB), 1) % 2
        sel[...] = jnp.where(keep, full, 0.0).astype(BF16)

    def choose_ancestors(start, stop):
        if start == 0:
            local_ba.wait()
        block = iota((WIDE, WIDE), 0), iota((WIDE, WIDE), 1)
        earlier = ((block[0] // NB == block[1] // NB) & (block[0] < block[1])).astype(F32)
        earlier = earlier.astype(BF16)
        slot = iota((4 * 16, WIDE), 0)
        wanted = slot - slot % 2

        @pl.loop(start, stop)
        def _(b):
            owners = own_s[b]
            mine = jnp.max((owners == me).astype(F32), 0, keepdims=True)
            rank = nn(jnp.broadcast_to(mine, (8, WIDE)).astype(BF16), earlier)[0:1, :]
            base = (iota((1, WIDE), 1) // NB * 4).astype(F32)
            key = jnp.where(mine > 0, base + 2 * rank, -8.0)
            hit = key == wanted.astype(F32)
            acc = jnp.zeros((4 * 16, 128), F32)
            for parity in range(2):
                one = (hit & (slot % 2 == parity)).astype(F32).astype(BF16)
                v = ba[pl.ds(b * 2 * WIDE + parity, WIDE, stride=2), :]
                hi, low = split(v)
                acc = acc + nn(one, hi) + nn(one, low)
            ba4[rows_of(b * 64, 64), :] = acc

    def exchange(n):
        h = halves[n]
        v = ld[h]
        hi, low = split(v)
        rest = (v - hi.astype(F32) - low.astype(F32)).astype(BF16)
        packed = nn(sel[...], hi) + nn(sel[...], low) + nn(sel[...], rest)
        pk[n] = packed.reshape(DEV, 4, 128)
        got[h, group] = pk[n, me]
        for i in range(1, DEV):
            p, r, c = (pole + i // 16) % 8, (row + i // 4) % 4, (col + i) % 4
            pltpu.make_async_remote_copy(
                src_ref=pk.at[n, (p * 4 + r) * 4 + c], dst_ref=got.at[h, group],
                send_sem=asend.at[n], recv_sem=arecv.at[h],
                device_id=(p, r, c), device_id_type=MESH,
            ).start()

    def three(a, b):
        ahi, alo = split(a)
        bhi, blo = split(b)
        return nn(ahi, bhi) + nn(ahi, blo) + nn(alo, bhi)

    for b in range(1, 4):
        split_a(b)
    local_l.wait()
    l_near[0].wait_recv()
    chunk(0, 0)
    l_near[1].wait_recv()
    chunk(0, 1)
    l_near[2].wait_recv()
    chunk(0, 2)
    ls = [l_share(0, lo[0])]
    lower_term(0)
    zn = ring1(0, z_ring)
    choose_rows()
    choose_ancestors(0, 4)
    uf_moves = [u_forward(0, uo[0])]
    ls[0].wait_recv()
    chunk(1, 0)
    zn = ring2(0, z_ring, zn)
    ls.append(l_share(1, lo[1]))
    choose_ancestors(4, 8)
    ls.append(l_share(2, lo[2]))
    uf_moves.append(u_forward(1, uo[1]))
    uf_moves.append(u_forward(2, uo[2]))
    local_u.wait()
    ls[1].wait_recv()
    chunk(1, 1)
    ring3(0, z_ring, zn)
    yn = y_send(0)
    ls[2].wait_recv()
    chunk(1, 2)
    lower_term(1)
    zf = ring1(1, z_ring)
    for h in range(2):
        hs = pl.ds(h * 128, 128)
        hi, low = split(xi[h])
        xih[:, hs], xil[:, hs] = hi, low
        hi, low = split(xr[h])
        xrh[:, hs], xrl[:, hs] = hi, low
    for c in uf_moves[0]:
        c.wait_recv()
    upper_prep(0)
    upper_chunk(0)
    y_sum(0, yn)
    xn = x_swap(0)
    pivot_chunk(0)
    zf = ring2(1, z_ring, zf)
    for c in uf_moves[1]:
        c.wait_recv()
    upper_prep(1)
    pivot_chunk(1)
    for c in uf_moves[2]:
        c.wait_recv()
    upper_prep(2)
    pivot_chunk(2)

    place = (iota((Q, S), 1) == iota((Q, S), 0) + col * Q).astype(F32)
    piece = w_re * piv_ref[0, 1] + w_im * piv_ref[0, 0]
    placed = jnp.dot(piece, place, precision=lax.Precision.HIGHEST, preferred_element_type=F32)
    for g in range(32):
        at = (g % 2, (g // 4) % 4, ((g // 2) % 2) * 2 + g // 16)
        mine = (row == g // 8).astype(F32)
        pvb[at[0], at[1], at[2]] = (
            pvs[g * 8 : g * 8 + 8, :] + mine * placed[(g % 8) * 8 : (g % 8) * 8 + 8, :]
        )
    p1 = send(pvb.at[1 - core], pc, d_core)
    x_add(0, xn)
    exchange(0)
    p1.wait_recv()
    pvb[core] += pc[...]

    def in_plane(n):
        zz, xx = (z + n // 4) % 4, (x + n) % 4
        return zz, xx, ((xx % 2) * 4 + zz, (xx // 2) * 2 + core, col)

    p2 = []
    for n in range(1, 16):
        zz, xx, dev = in_plane(n)
        p2.append(send(pvb.at[core, zz, xx], pz.at[n - 1], dev))
    upper_chunk(1)
    ring3(1, z_ring, zf)
    yf = y_send(1)
    upper_chunk(2)
    for g in range(32):
        at = (g % 2, (g // 4) % 4, ((g // 2) % 2) * 2 + g // 16)
        cb[at[0], at[1], at[2]] = -y[g * 8 : g * 8 + 8, :]
    to_core = send(cb.at[1 - core], rc, d_core)
    for c in p2:
        c.wait_recv()
    pb[col] = pvb[core, z, x] + jnp.sum(pz[...], 0)
    p4 = [send(pb.at[col], pb.at[col], at_y((col + d) % 4)) for d in range(1, 4)]
    for g in range(32):
        k = (g % 2) * 16 + ((g // 4) % 4) * 4 + ((g // 2) % 2) * 2 + g // 16
        bsp[k * 8 : k * 8 + 8, :] = bs_ref[g * 8 : g * 8 + 8, :]
    to_core.wait_recv()

    @pl.loop(0, 4)
    def _(b):
        cb[core, b] += rc[b]

    y_sum(1, yf)
    xf = x_swap(1)

    wide, rest = pl.ds(0, LEFT), pl.ds(LEFT, T - LEFT)
    fa = [
        send(cb.at[core, (z + d) % 4, :, :, wide], ra.at[d - 1], at_z((z + d) % 4))
        for d in range(1, 4)
    ]
    fb = [
        send(cb.at[core, :, (x + d) % 4, :, rest], rb.at[d - 1], at_x((x + d) % 4))
        for d in range(1, 4)
    ]
    for c in p4:
        c.wait_recv()
    pfull[core, z, x] = pb[0] + pb[1] + pb[2] + pb[3]
    p5 = []
    for n in range(1, 16):
        zz, xx, dev = in_plane(n)
        p5.append(send(pfull.at[core, z, x], pfull.at[core, z, x], dev))
    x_add(1, xf)
    exchange(1)
    for c in fb:
        c.wait_recv()
    cb[core, :, x, :, LEFT:] += rb[0] + rb[1] + rb[2]
    hb = [
        send(cb.at[core, (z + d) % 4, x, :, rest], rv.at[d - 1, :, rest], at_z((z + d) % 4))
        for d in range(1, 4)
    ]
    for c in fa:
        c.wait_recv()
    cb[core, z, :, :, :LEFT] += ra[0] + ra[1] + ra[2]
    ha = [
        send(cb.at[core, z, (x + d) % 4, :, wide], rv.at[d - 1, :, wide], at_x((x + d) % 4))
        for d in range(1, 4)
    ]
    for c in p5:
        c.wait_recv()
    p6 = send(pfull.at[core], pfull.at[core], d_core)
    for c in hb + ha:
        c.wait_recv()
    out_ref[:, :T] = cb[core, z, x] + rv[0] + rv[1] + rv[2]
    p6.wait_recv()
    pivot = pfull[...].reshape(S, S)
    charge = jnp.sum(bsp[...] * three(pivot, bs_ref[...]), 0, keepdims=True)
    others = pl.ds(0, DEV - 1)
    for h in range(2):
        pltpu.make_async_copy(got.at[h, others], got.at[h, others], arecv.at[h]).wait()
    received = jnp.concatenate([got[h].reshape(4 * DEV, 128) for h in range(2)], 1)
    projected = three(received, bs_ref[...])
    charge = charge + jnp.sum(ba4[...] * projected, 0, keepdims=True)
    out_ref[:, T:] = jnp.broadcast_to(charge, (8, 128))
    for n in range(2):
        pltpu.make_async_copy(pk.at[n, others], pk.at[n, others], asend.at[n]).wait()
    for c in started:
        c.wait_send()


N_COPIES = 112


def hand_out(both_ref, upper_ref, charge_ref):
    upper_ref[...] = both_ref[:, :T]
    charge_ref[...] = both_ref[0:1, T:]


def fused(weights, tile, lower, upper, pivot, owners, basis_super, basis_ancestor):
    vmem = pl.BlockSpec(memory_space=pltpu.VMEM)
    hbm = pl.BlockSpec(memory_space=pl.ANY)
    return pl.pallas_call(
        kernel,
        out_shape=jax.ShapeDtypeStruct((8, T + 128), F32),
        in_specs=[pl.BlockSpec(memory_space=pltpu.SMEM), hbm, hbm, hbm, vmem, vmem, vmem, hbm],
        out_specs=vmem,
        scratch_shapes=[
            pltpu.VMEM((2, T, T), F32),
            pltpu.VMEM((2, T, T), BF16),
            pltpu.VMEM((2, T, T), BF16),
            pltpu.VMEM((4, 2, Q, T), F32),
            pltpu.VMEM((4, 2, Q, T), F32),
            pltpu.VMEM((4, S, T), BF16),
            pltpu.VMEM((4, S, T), BF16),
            pltpu.VMEM((2, S, T), BF16),
            pltpu.VMEM((2, S, T), BF16),
            pltpu.VMEM((2, T, 128), F32),
            pltpu.VMEM((2, T, 128), F32),
            pltpu.VMEM((T, S), BF16),
            pltpu.VMEM((T, S), BF16),
            pltpu.VMEM((T, S), BF16),
            pltpu.VMEM((T, S), BF16),
            pltpu.VMEM((S, T), F32),
            pltpu.VMEM((2, T, 128), F32),
            pltpu.VMEM((2, BLK, 128), F32),
            pltpu.VMEM((2, 2, BLK, 128), F32),
            pltpu.VMEM((2, 3, SUB, 128), F32),
            pltpu.VMEM((2, SUB, 128), F32),
            pltpu.VMEM((2, SUB, 128), F32),
            pltpu.VMEM((2, 4, 4, 8, T), F32),
            pltpu.VMEM((4, 4, 8, T), F32),
            pltpu.VMEM((3, 4, 8, LEFT), F32),
            pltpu.VMEM((3, 4, 8, T - LEFT), F32),
            pltpu.VMEM((3, 8, T), F32),
            pltpu.VMEM((2, 4, 4, 8, S), F32),
            pltpu.VMEM((4, 4, 8, S), F32),
            pltpu.VMEM((15, 8, S), F32),
            pltpu.VMEM((4, 8, S), F32),
            pltpu.VMEM((2, 4, 4, 8, S), F32),
            pltpu.VMEM((S, 128), F32),
            pltpu.VMEM((4608, 128), F32),
            pltpu.VMEM((4 * DEV, 128), F32),
            pltpu.VMEM((4 * DEV, SUB), BF16),
            pltpu.VMEM((2, DEV, 4, 128), F32),
            pltpu.VMEM((2, DEV, 4, 128), F32),
            pltpu.VMEM((BAT, TOPK, WIDE), jnp.int32),
            pltpu.VMEM((S, S), F32),
            pltpu.VMEM((T, S), BF16),
            pltpu.VMEM((T, S), BF16),
            pltpu.VMEM((2, S, S), BF16),
            pltpu.SemaphoreType.DMA((N_COPIES,)),
            pltpu.SemaphoreType.DMA((N_COPIES,)),
            pltpu.SemaphoreType.DMA((7,)),
            pltpu.SemaphoreType.DMA((2,)),
            pltpu.SemaphoreType.DMA((2,)),
        ],
        compiler_params=pltpu.CompilerParams(
            collective_id=0, has_side_effects=True, vmem_limit_bytes=63 << 20
        ),
    )(weights, tile, lower, upper, pivot, owners, basis_super, basis_ancestor)


def body(
    inverse_tile, lower_factor, upper_factor, pivot_inverse, pole_weights, block_owners,
    basis_ancestor, basis_super,
):
    out = fused(
        pole_weights, inverse_tile, lower_factor, upper_factor, pivot_inverse, block_owners.T,
        basis_super, basis_ancestor,
    )
    upper_density, charge = pl.pallas_call(
        hand_out,
        out_shape=(jax.ShapeDtypeStruct((8, T), F32), jax.ShapeDtypeStruct((1, 128), F32)),
    )(out)
    return (upper_density, charge.reshape(128))


def solution(mesh):
    placed = (
        P("pole", None, "row", "col"),
        P("pole", None, "row", "col"),
        P("pole", None, "col", "row"),
        P("pole", None, "row", "col"),
        P("pole", None),
        P(),
        P(None, ("pole", "row", "col")),
        P(None, ("pole", "row", "col")),
    )
    return jax.shard_map(
        body,
        mesh=mesh,
        in_specs=placed,
        out_specs=(P(("pole", "row"), "col"), P(("pole", "row", "col"))),
        check_vma=False,
    )
```

```python
import jax
import jax.numpy as jnp
from jax import lax
from jax.experimental import pallas as pl
from jax.experimental.pallas import tpu as pltpu
from jax.sharding import PartitionSpec as P

MESH = pl.DeviceIdType.MESH
F32 = jnp.float32
BF16 = jnp.bfloat16
T = 1152
S = 256
Q = 64
NB = 18
TOPK = 6
BAT = 8
WIDE = 288
DEV = 128
CHUNKS = ((0, 512), (512, 512), (1024, 128))
BLK = 288
SUB = 72
TAIL = 1024
LEFT = 640


def nt(a, b):
    return lax.dot_general(a, b, (((1,), (1,)), ((), ())), preferred_element_type=F32)


def nn(a, b):
    return jnp.dot(a, b, preferred_element_type=F32)


def split(v):
    hi = v.astype(BF16)
    return hi, (v - hi.astype(F32)).astype(BF16)


def tn(a, b):
    return lax.dot_general(a, b, (((0,), (0,)), ((), ())), preferred_element_type=F32)


def iota(shape, dim):
    return lax.broadcasted_iota(jnp.int32, shape, dim)


def rows_of(start, size):
    return pl.ds(pl.multiple_of(start, 8), size)


def kernel(
    w_ref, a_hbm, l_hbm, u_hbm, piv_ref, own_ref, bs_ref, ba_hbm,
    out_ref,
    a32, ah, al, lf, uf, bl, br, uph, upl, xr, xi, xih, xil, xrh, xrl, y, lt,
    rz1, rz2, ry, rx, ld, cb, rc, ra, rb, rv,
    pvb, pc, pz, pb, pfull, bsp, ba, ba4, sel, pk, got, own_s, pvs, ath, atl, bt,
    sends, recvs, locs, asend, arecv,
):
    pole, row, col = lax.axis_index("pole"), lax.axis_index("row"), lax.axis_index("col")
    x_lo, z = pole // 4, pole % 4
    x_hi, core = row // 2, row % 2
    x = x_hi * 2 + x_lo
    me = (pole * 4 + row) * 4 + col
    group = row * 32 + z * 8 + col * 2 + x_lo

    def at_x(v):
        return ((v % 2) * 4 + z, (v // 2) * 2 + core, col)

    def at_y(v):
        return (pole, row, v)

    def at_z(v):
        return (x_lo * 4 + v, row, col)

    def row_x(v):
        return (v // 2) * 2 + core

    xp, xm, x2 = (x + 1) % 4, (x + 3) % 4, (x + 2) % 4
    yp, ym, y2 = (col + 1) % 4, (col + 3) % 4, (col + 2) % 4
    zp, zm, z2 = (z + 1) % 4, (z + 3) % 4, (z + 2) % 4
    d_core = (pole, x_hi * 2 + 1 - core, col)
    d_xp, d_xm = at_x(xp), at_x(xm)
    d_yp, d_ym = at_y(yp), at_y(ym)
    d_zp, d_zm = at_z(zp), at_z(zm)
    d_xn = at_x(x_hi * 2 + 1 - x_lo)
    started = []

    def send(src, dst, dev):
        n = len(started)
        c = pltpu.make_async_remote_copy(
            src_ref=src, dst_ref=dst, send_sem=sends.at[n], recv_sem=recvs.at[n],
            device_id=dev, device_id_type=MESH,
        )
        c.start()
        started.append(c)
        return c

    local_a = []
    for b in range(4):
        rs = slice(b * BLK, (b + 1) * BLK)
        c = pltpu.make_async_copy(a_hbm.at[0, :, rs, :], a32.at[:, rs, :], locs.at[b])
        local_a.append(c)
    local_l = pltpu.make_async_copy(l_hbm.at[0], lf.at[row], locs.at[4])
    local_u = pltpu.make_async_copy(u_hbm.at[0], uf.at[col], locs.at[5])
    local_ba = pltpu.make_async_copy(ba_hbm, ba, locs.at[6])
    local_l.start()
    for c in local_a:
        c.start()

    def split_a(b):
        local_a[b].wait()

        @pl.loop(0, BLK // 16)
        def _(i):
            rs = pl.ds(pl.multiple_of(b * BLK + i * 16, 16), 16)
            for part in range(2):
                hi, low = split(a32[part, rs, :])
                ah[part, rs, :] = hi
                al[part, rs, :] = low
                ath[rs, part * 128 : part * 128 + 128] = hi[:, TAIL:]
                atl[rs, part * 128 : part * 128 + 128] = low[:, TAIL:]

    barrier = pltpu.get_barrier_semaphore()
    greet = (d_core, d_xp, d_xm, at_x(x2), d_yp, d_ym, d_zp, d_zm)
    for dev in greet:
        pl.semaphore_signal(barrier, inc=1, device_id=dev, device_id_type=MESH)
    split_a(0)
    pl.semaphore_wait(barrier, len(greet))

    def lanes(k):
        return pl.ds(CHUNKS[k][0], CHUNKS[k][1])

    def l_own(k):
        return send(l_hbm.at[0, :, :, lanes(k)], lf.at[row, :, :, lanes(k)], at_x(x2))

    far = (1 - x_hi) * 2 + core

    def l_share(k, own):
        own.wait_recv()
        return send(lf.at[far, :, :, lanes(k)], lf.at[far, :, :, lanes(k)], d_core)

    def u_own(k):
        return (
            send(u_hbm.at[0, :, :, lanes(k)], uf.at[col, :, :, lanes(k)], d_yp),
            send(u_hbm.at[0, :, :, lanes(k)], uf.at[col, :, :, lanes(k)], d_ym),
        )

    def u_forward(k, own):
        own[0].wait_recv()
        p = send(uf.at[ym, 0, :, lanes(k)], uf.at[ym, 0, :, lanes(k)], d_yp)
        own[1].wait_recv()
        m = send(uf.at[yp, 1, :, lanes(k)], uf.at[yp, 1, :, lanes(k)], d_ym)
        return p, m

    l_near, lo, uo = [], [], []
    for k in range(3):
        l_near.append(send(l_hbm.at[0, :, :, lanes(k)], lf.at[row, :, :, lanes(k)], d_core))
        lo.append(l_own(k))
        uo.append(u_own(k))
    local_ba.start()
    local_u.start()

    w_re, w_im = w_ref[0, 0], w_ref[0, 1]

    def build(dst, slot, q, lane):
        re, im = lf[slot, 0, :, lane], lf[slot, 1, :, lane]
        a, b = pl.ds(q * Q, Q), pl.ds(2 * Q + q * Q, Q)
        rh, rl = split(re)
        ih, il = split(im)
        if lane.start == TAIL:
            one, two = pl.ds(0, 128), pl.ds(128, 128)
            bt[0, a, one], bt[1, a, one] = rh, rl
            bt[0, b, one], bt[1, b, one] = ih, il
            bt[0, a, two], bt[1, a, two] = -ih, -il
            bt[0, b, two], bt[1, b, two] = rh, rl
            return
        dst[0, a, lane], dst[1, a, lane] = rh, rl
        dst[0, b, lane], dst[1, b, lane] = ih, il
        dst[2, a, lane], dst[3, a, lane] = -ih, -il
        dst[2, b, lane], dst[3, b, lane] = rh, rl

    def product(rs, lane, b):
        acc = nt(ah[0, rs, lane], b[0, :, lane])
        acc = acc + nt(ah[0, rs, lane], b[1, :, lane])
        acc = acc + nt(al[0, rs, lane], b[0, :, lane])
        acc = acc + nt(ah[1, rs, lane], b[2, :, lane])
        acc = acc + nt(ah[1, rs, lane], b[3, :, lane])
        acc = acc + nt(al[1, rs, lane], b[2, :, lane])
        return acc

    halves = (x_hi, 1 - x_hi)

    def lower_term(n):
        h = halves[n]

        @pl.loop(0, 4)
        def _(b):
            rs = pl.ds(pl.multiple_of(b * BLK, 16), BLK)
            lt[h, rs, :] = -(w_re * xi[h, rs, :] + w_im * xr[h, rs, :])

    def z_at(b):
        return b * BLK

    def y_at(b):
        return z * BLK + b * SUB

    z_ring = (z_at, BLK, 144, (zp, zm, z2, z), (d_zp, d_zm), rz1, rz2)

    def y_send(n):
        h = halves[n]
        return [
            send(lt.at[h, rows_of(y_at((col + d) % 4), SUB), :], ry.at[n, d - 1], at_y((col + d) % 4))
            for d in range(1, 4)
        ]

    def y_sum(n, before):
        for c in before:
            c.wait_recv()
        lt[halves[n], rows_of(y_at(col), SUB), :] += ry[n, 0] + ry[n, 1] + ry[n, 2]

    def ring1(n, ring):
        at, size, first, (p, m, two, own), (dp, dm), r1, r2 = ring
        h = halves[n]
        return (
            send(lt.at[h, rows_of(at(two), first), :], r1.at[n, pl.ds(0, first), :], dp),
            send(
                lt.at[h, rows_of(at(two) + first, size - first), :],
                r1.at[n, pl.ds(first, size - first), :], dm,
            ),
        )

    def ring2(n, ring, before):
        at, size, first, (p, m, two, own), (dp, dm), r1, r2 = ring
        h = halves[n]
        before[0].wait_recv()
        lt[h, rows_of(at(p), first), :] += r1[n, 0:first]
        a = send(lt.at[h, rows_of(at(p), size), :], r2.at[n, 0], dp)
        before[1].wait_recv()
        lt[h, rows_of(at(m) + first, size - first), :] += r1[n, first:size]
        return a, send(lt.at[h, rows_of(at(m), size), :], r2.at[n, 1], dm)

    def ring3(n, ring, before):
        at, size, first, (p, m, two, own), (dp, dm), r1, r2 = ring
        before[0].wait_recv()
        before[1].wait_recv()
        lt[halves[n], rows_of(at(own), size), :] += r2[n, 0] + r2[n, 1]

    def x_swap(n):
        return send(lt.at[halves[n], rows_of(y_at(col), SUB), :], rx.at[n], d_xn)

    def x_add(n, before):
        before.wait_recv()
        ld[halves[n]] = lt[halves[n], rows_of(y_at(col), SUB), :] + rx[n]

    def upper_prep(k):
        lane = lanes(k)
        for q in range(4):
            re, im = uf[q, 0, :, lane], uf[q, 1, :, lane]
            rs = pl.ds(q * Q, Q)
            for part, v in ((0, w_re * re - w_im * im), (1, w_re * im + w_im * re)):
                hi, low = split(v)
                uph[part, rs, lane] = hi
                upl[part, rs, lane] = low

    def upper_chunk(k, parts=(0, 1)):
        lane = lanes(k)
        acc = None
        for part in parts:
            for left, right in ((uph, ah), (uph, al), (upl, ah)):
                one = nn(left[part, :, lane], right[1 - part, lane, :])
                acc = one if acc is None else acc + one
        if k == 0:
            y[...] = acc
        else:
            y[...] += acc

    def chunk(n, k, blocks=(0, 4)):
        dst, h = ((bl, br)[n], halves[n])
        if blocks[0] == 0:
            for q in range(2):
                build(dst, h * 2 + q, q, lanes(k))

        @pl.loop(*blocks)
        def _(b):
            rs = pl.ds(pl.multiple_of(b * BLK, 16), BLK)
            if k == 2:
                acc = nt(ath[rs, :], bt[0]) + nt(ath[rs, :], bt[1]) + nt(atl[rs, :], bt[0])
            else:
                acc = product(rs, lanes(k), dst)
            if k == 0:
                xr[h, rs, :] = acc[:, :128]
                xi[h, rs, :] = acc[:, 128:]
            else:
                xr[h, rs, :] += acc[:, :128]
                xi[h, rs, :] += acc[:, 128:]

    def pivot_chunk(k):
        lane = lanes(k)
        acc = nn(uph[0, :, lane], xih[lane, :])
        acc = acc + nn(uph[0, :, lane], xil[lane, :])
        acc = acc + nn(upl[0, :, lane], xih[lane, :])
        acc = acc + nn(uph[1, :, lane], xrh[lane, :])
        acc = acc + nn(uph[1, :, lane], xrl[lane, :])
        acc = acc + nn(upl[1, :, lane], xrh[lane, :])
        if k == 0:
            pvs[...] = acc
        else:
            pvs[...] += acc

    def choose_rows():
        for b in range(BAT):
            own_s[b] = own_ref[:, b * WIDE : (b + 1) * WIDE]
        mine = own_s[group // 16].astype(F32).astype(BF16)
        here = nn(
            mine,
            (iota((WIDE, NB), 0) == (group % 16) * NB + iota((WIDE, NB), 1)).astype(F32).astype(BF16),
        )
        owner = iota((2 * DEV, NB), 0)
        named = jnp.zeros((2 * DEV, NB), F32)
        for t in range(TOPK):
            hit = here[t : t + 1, :] == (owner // 2).astype(F32)
            named = jnp.maximum(named, hit.astype(F32))
        earlier = (iota((NB, NB), 0) < iota((NB, NB), 1)).astype(F32).astype(BF16)
        rank = nn(named.astype(BF16), earlier)
        chosen = named * (rank == (owner % 2).astype(F32)).astype(F32)
        spot = iota((NB, SUB), 1)
        spread = (
            (spot // 36 == x_lo) & ((spot % 36) // 2 == iota((NB, SUB), 0))
        ).astype(F32)
        wide = nn(chosen.astype(BF16), spread.astype(BF16))
        out = iota((4 * DEV, 2 * DEV), 0)
        repeat = (iota((4 * DEV, 2 * DEV), 1) == out // 2).astype(F32)
        full = nn(repeat.astype(BF16), wide.astype(BF16))
        keep = iota((4 * DEV, SUB), 0) % 2 == iota((4 * DEV, SUB), 1) % 2
        sel[...] = jnp.where(keep, full, 0.0).astype(BF16)

    def choose_ancestors(start, stop):
        if start == 0:
            local_ba.wait()
        block = iota((WIDE, WIDE), 0), iota((WIDE, WIDE), 1)
        earlier = ((block[0] // NB == block[1] // NB) & (block[0] < block[1])).astype(F32)
        earlier = earlier.astype(BF16)
        slot = iota((4 * 16, WIDE), 0)
        wanted = slot - slot % 2

        @pl.loop(start, stop)
        def _(b):
            owners = own_s[b]
            mine = jnp.max((owners == me).astype(F32), 0, keepdims=True)
            rank = nn(jnp.broadcast_to(mine, (8, WIDE)).astype(BF16), earlier)[0:1, :]
            base = (iota((1, WIDE), 1) // NB * 4).astype(F32)
            key = jnp.where(mine > 0, base + 2 * rank, -8.0)
            hit = key == wanted.astype(F32)
            acc = jnp.zeros((4 * 16, 128), F32)
            for parity in range(2):
                one = (hit & (slot % 2 == parity)).astype(F32).astype(BF16)
                v = ba[pl.ds(b * 2 * WIDE + parity, WIDE, stride=2), :]
                hi, low = split(v)
                acc = acc + nn(one, hi) + nn(one, low)
            ba4[rows_of(b * 64, 64), :] = acc

    def exchange(n):
        h = halves[n]
        v = ld[h]
        hi, low = split(v)
        rest = (v - hi.astype(F32) - low.astype(F32)).astype(BF16)
        packed = nn(sel[...], hi) + nn(sel[...], low) + nn(sel[...], rest)
        pk[n] = packed.reshape(DEV, 4, 128)
        got[h, group] = pk[n, me]
        for i in range(1, DEV):
            p, r, c = (pole + i // 16) % 8, (row + i // 4) % 4, (col + i) % 4
            pltpu.make_async_remote_copy(
                src_ref=pk.at[n, (p * 4 + r) * 4 + c], dst_ref=got.at[h, group],
                send_sem=asend.at[n], recv_sem=arecv.at[h],
                device_id=(p, r, c), device_id_type=MESH,
            ).start()

    def three(a, b):
        ahi, alo = split(a)
        bhi, blo = split(b)
        return nn(ahi, bhi) + nn(ahi, blo) + nn(alo, bhi)

    for b in range(1, 4):
        split_a(b)
    local_l.wait()
    l_near[0].wait_recv()
    chunk(0, 0)
    l_near[1].wait_recv()
    chunk(0, 1)
    l_near[2].wait_recv()
    chunk(0, 2)
    ls = [l_share(0, lo[0])]
    lower_term(0)
    zn = ring1(0, z_ring)
    choose_rows()
    choose_ancestors(0, 4)
    uf_moves = [u_forward(0, uo[0])]
    ls[0].wait_recv()
    chunk(1, 0)
    zn = ring2(0, z_ring, zn)
    ls.append(l_share(1, lo[1]))
    choose_ancestors(4, 8)
    ls.append(l_share(2, lo[2]))
    local_u.wait()
    ls[1].wait_recv()
    chunk(1, 1)
    uf_moves.append(u_forward(1, uo[1]))
    uf_moves.append(u_forward(2, uo[2]))
    ring3(0, z_ring, zn)
    yn = y_send(0)
    ls[2].wait_recv()
    chunk(1, 2)
    lower_term(1)
    zf = ring1(1, z_ring)
    for h in range(2):
        hs = pl.ds(h * 128, 128)
        hi, low = split(xi[h])
        xih[:, hs], xil[:, hs] = hi, low
        hi, low = split(xr[h])
        xrh[:, hs], xrl[:, hs] = hi, low
    for c in uf_moves[0]:
        c.wait_recv()
    upper_prep(0)
    upper_chunk(0)
    y_sum(0, yn)
    xn = x_swap(0)
    pivot_chunk(0)
    zf = ring2(1, z_ring, zf)
    for c in uf_moves[1]:
        c.wait_recv()
    upper_prep(1)
    pivot_chunk(1)
    for c in uf_moves[2]:
        c.wait_recv()
    upper_prep(2)
    pivot_chunk(2)

    place = (iota((Q, S), 1) == iota((Q, S), 0) + col * Q).astype(F32)
    piece = w_re * piv_ref[0, 1] + w_im * piv_ref[0, 0]
    placed = jnp.dot(piece, place, precision=lax.Precision.HIGHEST, preferred_element_type=F32)
    for g in range(32):
        at = (g % 2, (g // 4) % 4, ((g // 2) % 2) * 2 + g // 16)
        mine = (row == g // 8).astype(F32)
        pvb[at[0], at[1], at[2]] = (
            pvs[g * 8 : g * 8 + 8, :] + mine * placed[(g % 8) * 8 : (g % 8) * 8 + 8, :]
        )
    p1 = send(pvb.at[1 - core], pc, d_core)
    x_add(0, xn)
    exchange(0)
    p1.wait_recv()
    pvb[core] += pc[...]

    def in_plane(n):
        zz, xx = (z + n // 4) % 4, (x + n) % 4
        return zz, xx, ((xx % 2) * 4 + zz, (xx // 2) * 2 + core, col)

    p2 = []
    for n in range(1, 16):
        zz, xx, dev = in_plane(n)
        p2.append(send(pvb.at[core, zz, xx], pz.at[n - 1], dev))
    upper_chunk(1)
    ring3(1, z_ring, zf)
    yf = y_send(1)
    upper_chunk(2)
    for g in range(32):
        at = (g % 2, (g // 4) % 4, ((g // 2) % 2) * 2 + g // 16)
        cb[at[0], at[1], at[2]] = -y[g * 8 : g * 8 + 8, :]
    to_core = send(cb.at[1 - core], rc, d_core)
    for c in p2:
        c.wait_recv()
    pb[col] = pvb[core, z, x] + jnp.sum(pz[...], 0)
    p4 = [send(pb.at[col], pb.at[col], at_y((col + d) % 4)) for d in range(1, 4)]
    for g in range(32):
        k = (g % 2) * 16 + ((g // 4) % 4) * 4 + ((g // 2) % 2) * 2 + g // 16
        bsp[k * 8 : k * 8 + 8, :] = bs_ref[g * 8 : g * 8 + 8, :]
    to_core.wait_recv()

    @pl.loop(0, 4)
    def _(b):
        cb[core, b] += rc[b]

    y_sum(1, yf)
    xf = x_swap(1)

    wide, rest = pl.ds(0, LEFT), pl.ds(LEFT, T - LEFT)
    fa = [
        send(cb.at[core, (z + d) % 4, :, :, wide], ra.at[d - 1], at_z((z + d) % 4))
        for d in range(1, 4)
    ]
    fb = [
        send(cb.at[core, :, (x + d) % 4, :, rest], rb.at[d - 1], at_x((x + d) % 4))
        for d in range(1, 4)
    ]
    for c in p4:
        c.wait_recv()
    pfull[core, z, x] = pb[0] + pb[1] + pb[2] + pb[3]
    p5 = []
    for n in range(1, 16):
        zz, xx, dev = in_plane(n)
        p5.append(send(pfull.at[core, z, x], pfull.at[core, z, x], dev))
    x_add(1, xf)
    exchange(1)
    for c in fb:
        c.wait_recv()
    cb[core, :, x, :, LEFT:] += rb[0] + rb[1] + rb[2]
    hb = [
        send(cb.at[core, (z + d) % 4, x, :, rest], rv.at[d - 1, :, rest], at_z((z + d) % 4))
        for d in range(1, 4)
    ]
    for c in fa:
        c.wait_recv()
    cb[core, z, :, :, :LEFT] += ra[0] + ra[1] + ra[2]
    ha = [
        send(cb.at[core, z, (x + d) % 4, :, wide], rv.at[d - 1, :, wide], at_x((x + d) % 4))
        for d in range(1, 4)
    ]
    for c in p5:
        c.wait_recv()
    p6 = send(pfull.at[core], pfull.at[core], d_core)
    for c in hb + ha:
        c.wait_recv()
    out_ref[:, :T] = cb[core, z, x] + rv[0] + rv[1] + rv[2]
    p6.wait_recv()
    pivot = pfull[...].reshape(S, S)
    charge = jnp.sum(bsp[...] * three(pivot, bs_ref[...]), 0, keepdims=True)
    others = pl.ds(0, DEV - 1)
    for h in range(2):
        pltpu.make_async_copy(got.at[h, others], got.at[h, others], arecv.at[h]).wait()
    received = jnp.concatenate([got[h].reshape(4 * DEV, 128) for h in range(2)], 1)
    projected = three(received, bs_ref[...])
    charge = charge + jnp.sum(ba4[...] * projected, 0, keepdims=True)
    out_ref[:, T:] = jnp.broadcast_to(charge, (8, 128))
    for n in range(2):
        pltpu.make_async_copy(pk.at[n, others], pk.at[n, others], asend.at[n]).wait()
    for c in started:
        c.wait_send()


N_COPIES = 112


def hand_out(both_ref, upper_ref, charge_ref):
    upper_ref[...] = both_ref[:, :T]
    charge_ref[...] = both_ref[0:1, T:]


def fused(weights, tile, lower, upper, pivot, owners, basis_super, basis_ancestor):
    vmem = pl.BlockSpec(memory_space=pltpu.VMEM)
    hbm = pl.BlockSpec(memory_space=pl.ANY)
    return pl.pallas_call(
        kernel,
        out_shape=jax.ShapeDtypeStruct((8, T + 128), F32),
        in_specs=[pl.BlockSpec(memory_space=pltpu.SMEM), hbm, hbm, hbm, vmem, vmem, vmem, hbm],
        out_specs=vmem,
        scratch_shapes=[
            pltpu.VMEM((2, T, T), F32),
            pltpu.VMEM((2, T, T), BF16),
            pltpu.VMEM((2, T, T), BF16),
            pltpu.VMEM((4, 2, Q, T), F32),
            pltpu.VMEM((4, 2, Q, T), F32),
            pltpu.VMEM((4, S, T), BF16),
            pltpu.VMEM((4, S, T), BF16),
            pltpu.VMEM((2, S, T), BF16),
            pltpu.VMEM((2, S, T), BF16),
            pltpu.VMEM((2, T, 128), F32),
            pltpu.VMEM((2, T, 128), F32),
            pltpu.VMEM((T, S), BF16),
            pltpu.VMEM((T, S), BF16),
            pltpu.VMEM((T, S), BF16),
            pltpu.VMEM((T, S), BF16),
            pltpu.VMEM((S, T), F32),
            pltpu.VMEM((2, T, 128), F32),
            pltpu.VMEM((2, BLK, 128), F32),
            pltpu.VMEM((2, 2, BLK, 128), F32),
            pltpu.VMEM((2, 3, SUB, 128), F32),
            pltpu.VMEM((2, SUB, 128), F32),
            pltpu.VMEM((2, SUB, 128), F32),
            pltpu.VMEM((2, 4, 4, 8, T), F32),
            pltpu.VMEM((4, 4, 8, T), F32),
            pltpu.VMEM((3, 4, 8, LEFT), F32),
            pltpu.VMEM((3, 4, 8, T - LEFT), F32),
            pltpu.VMEM((3, 8, T), F32),
            pltpu.VMEM((2, 4, 4, 8, S), F32),
            pltpu.VMEM((4, 4, 8, S), F32),
            pltpu.VMEM((15, 8, S), F32),
            pltpu.VMEM((4, 8, S), F32),
            pltpu.VMEM((2, 4, 4, 8, S), F32),
            pltpu.VMEM((S, 128), F32),
            pltpu.VMEM((4608, 128), F32),
            pltpu.VMEM((4 * DEV, 128), F32),
            pltpu.VMEM((4 * DEV, SUB), BF16),
            pltpu.VMEM((2, DEV, 4, 128), F32),
            pltpu.VMEM((2, DEV, 4, 128), F32),
            pltpu.VMEM((BAT, TOPK, WIDE), jnp.int32),
            pltpu.VMEM((S, S), F32),
            pltpu.VMEM((T, S), BF16),
            pltpu.VMEM((T, S), BF16),
            pltpu.VMEM((2, S, S), BF16),
            pltpu.SemaphoreType.DMA((N_COPIES,)),
            pltpu.SemaphoreType.DMA((N_COPIES,)),
            pltpu.SemaphoreType.DMA((7,)),
            pltpu.SemaphoreType.DMA((2,)),
            pltpu.SemaphoreType.DMA((2,)),
        ],
        compiler_params=pltpu.CompilerParams(
            collective_id=0, has_side_effects=True, vmem_limit_bytes=63 << 20
        ),
    )(weights, tile, lower, upper, pivot, owners, basis_super, basis_ancestor)


def body(
    inverse_tile, lower_factor, upper_factor, pivot_inverse, pole_weights, block_owners,
    basis_ancestor, basis_super,
):
    out = fused(
        pole_weights, inverse_tile, lower_factor, upper_factor, pivot_inverse, block_owners.T,
        basis_super, basis_ancestor,
    )
    upper_density, charge = pl.pallas_call(
        hand_out,
        out_shape=(jax.ShapeDtypeStruct((8, T), F32), jax.ShapeDtypeStruct((1, 128), F32)),
    )(out)
    return (upper_density, charge.reshape(128))


def solution(mesh):
    placed = (
        P("pole", None, "row", "col"),
        P("pole", None, "row", "col"),
        P("pole", None, "col", "row"),
        P("pole", None, "row", "col"),
        P("pole", None),
        P(),
        P(None, ("pole", "row", "col")),
        P(None, ("pole", "row", "col")),
    )
    return jax.shard_map(
        body,
        mesh=mesh,
        in_specs=placed,
        out_specs=(P(("pole", "row"), "col"), P(("pole", "row", "col"))),
        check_vma=False,
    )
```

```python
import jax
import jax.numpy as jnp
from jax import lax
from jax.experimental import pallas as pl
from jax.experimental.pallas import tpu as pltpu
from jax.sharding import PartitionSpec as P

MESH = pl.DeviceIdType.MESH
F32 = jnp.float32
BF16 = jnp.bfloat16
T = 1152
S = 256
Q = 64
NB = 18
TOPK = 6
BAT = 8
WIDE = 288
DEV = 128
CHUNKS = ((0, 512), (512, 512), (1024, 128))
BLK = 288
SUB = 72
TAIL = 1024
LEFT = 640


def nt(a, b):
    return lax.dot_general(a, b, (((1,), (1,)), ((), ())), preferred_element_type=F32)


def nn(a, b):
    return jnp.dot(a, b, preferred_element_type=F32)


def split(v):
    hi = v.astype(BF16)
    return hi, (v - hi.astype(F32)).astype(BF16)


def tn(a, b):
    return lax.dot_general(a, b, (((0,), (0,)), ((), ())), preferred_element_type=F32)


def iota(shape, dim):
    return lax.broadcasted_iota(jnp.int32, shape, dim)


def rows_of(start, size):
    return pl.ds(pl.multiple_of(start, 8), size)


def kernel(
    w_ref, a_hbm, l_hbm, u_hbm, piv_ref, own_ref, bs_ref, ba_hbm,
    out_ref,
    a32, ah, al, lf, uf, bl, br, uph, upl, xr, xi, xih, xil, xrh, xrl, y, lt,
    rz1, rz2, ry, rx, ld, cb, rc, ra, rb, rv,
    pvb, pc, pz, pb, pfull, bsp, ba, ba4, sel, pk, got, own_s, pvs, ath, atl, bt,
    sends, recvs, locs, asend, arecv,
):
    pole, row, col = lax.axis_index("pole"), lax.axis_index("row"), lax.axis_index("col")
    x_lo, z = pole // 4, pole % 4
    x_hi, core = row // 2, row % 2
    x = x_hi * 2 + x_lo
    me = (pole * 4 + row) * 4 + col
    group = row * 32 + z * 8 + col * 2 + x_lo

    def at_x(v):
        return ((v % 2) * 4 + z, (v // 2) * 2 + core, col)

    def at_y(v):
        return (pole, row, v)

    def at_z(v):
        return (x_lo * 4 + v, row, col)

    def row_x(v):
        return (v // 2) * 2 + core

    xp, xm, x2 = (x + 1) % 4, (x + 3) % 4, (x + 2) % 4
    yp, ym, y2 = (col + 1) % 4, (col + 3) % 4, (col + 2) % 4
    zp, zm, z2 = (z + 1) % 4, (z + 3) % 4, (z + 2) % 4
    d_core = (pole, x_hi * 2 + 1 - core, col)
    d_xp, d_xm = at_x(xp), at_x(xm)
    d_yp, d_ym = at_y(yp), at_y(ym)
    d_zp, d_zm = at_z(zp), at_z(zm)
    d_xn = at_x(x_hi * 2 + 1 - x_lo)
    started = []

    def send(src, dst, dev):
        n = len(started)
        c = pltpu.make_async_remote_copy(
            src_ref=src, dst_ref=dst, send_sem=sends.at[n], recv_sem=recvs.at[n],
            device_id=dev, device_id_type=MESH,
        )
        c.start()
        started.append(c)
        return c

    local_a = []
    for b in range(4):
        rs = slice(b * BLK, (b + 1) * BLK)
        c = pltpu.make_async_copy(a_hbm.at[0, :, rs, :], a32.at[:, rs, :], locs.at[b])
        local_a.append(c)
    local_l = pltpu.make_async_copy(l_hbm.at[0], lf.at[row], locs.at[4])
    local_u = pltpu.make_async_copy(u_hbm.at[0], uf.at[col], locs.at[5])
    local_ba = pltpu.make_async_copy(ba_hbm, ba, locs.at[6])
    local_l.start()
    for c in local_a:
        c.start()

    def split_a(b):
        local_a[b].wait()

        @pl.loop(0, BLK // 16)
        def _(i):
            rs = pl.ds(pl.multiple_of(b * BLK + i * 16, 16), 16)
            for part in range(2):
                hi, low = split(a32[part, rs, :])
                ah[part, rs, :] = hi
                al[part, rs, :] = low
                ath[rs, part * 128 : part * 128 + 128] = hi[:, TAIL:]
                atl[rs, part * 128 : part * 128 + 128] = low[:, TAIL:]

    barrier = pltpu.get_barrier_semaphore()
    greet = (d_core, d_xp, d_xm, at_x(x2), d_yp, d_ym, d_zp, d_zm)
    for dev in greet:
        pl.semaphore_signal(barrier, inc=1, device_id=dev, device_id_type=MESH)
    split_a(0)
    pl.semaphore_wait(barrier, len(greet))

    def lanes(k):
        return pl.ds(CHUNKS[k][0], CHUNKS[k][1])

    def l_own(k):
        return send(l_hbm.at[0, :, :, lanes(k)], lf.at[row, :, :, lanes(k)], at_x(x2))

    far = (1 - x_hi) * 2 + core

    def l_share(k, own):
        own.wait_recv()
        return send(lf.at[far, :, :, lanes(k)], lf.at[far, :, :, lanes(k)], d_core)

    def u_own(k):
        return (
            send(u_hbm.at[0, :, :, lanes(k)], uf.at[col, :, :, lanes(k)], d_yp),
            send(u_hbm.at[0, :, :, lanes(k)], uf.at[col, :, :, lanes(k)], d_ym),
        )

    def u_forward(k, own):
        own[0].wait_recv()
        p = send(uf.at[ym, 0, :, lanes(k)], uf.at[ym, 0, :, lanes(k)], d_yp)
        own[1].wait_recv()
        m = send(uf.at[yp, 1, :, lanes(k)], uf.at[yp, 1, :, lanes(k)], d_ym)
        return p, m

    l_near, lo, uo = [], [], []
    for k in range(3):
        l_near.append(send(l_hbm.at[0, :, :, lanes(k)], lf.at[row, :, :, lanes(k)], d_core))
        lo.append(l_own(k))
        uo.append(u_own(k))
    local_ba.start()
    local_u.start()

    w_re, w_im = w_ref[0, 0], w_ref[0, 1]

    def build(dst, slot, q, lane):
        re, im = lf[slot, 0, :, lane], lf[slot, 1, :, lane]
        a, b = pl.ds(q * Q, Q), pl.ds(2 * Q + q * Q, Q)
        rh, rl = split(re)
        ih, il = split(im)
        if lane.start == TAIL:
            one, two = pl.ds(0, 128), pl.ds(128, 128)
            bt[0, a, one], bt[1, a, one] = rh, rl
            bt[0, b, one], bt[1, b, one] = ih, il
            bt[0, a, two], bt[1, a, two] = -ih, -il
            bt[0, b, two], bt[1, b, two] = rh, rl
            return
        dst[0, a, lane], dst[1, a, lane] = rh, rl
        dst[0, b, lane], dst[1, b, lane] = ih, il
        dst[2, a, lane], dst[3, a, lane] = -ih, -il
        dst[2, b, lane], dst[3, b, lane] = rh, rl

    def product(rs, lane, b):
        acc = nt(ah[0, rs, lane], b[0, :, lane])
        acc = acc + nt(ah[0, rs, lane], b[1, :, lane])
        acc = acc + nt(al[0, rs, lane], b[0, :, lane])
        acc = acc + nt(ah[1, rs, lane], b[2, :, lane])
        acc = acc + nt(ah[1, rs, lane], b[3, :, lane])
        acc = acc + nt(al[1, rs, lane], b[2, :, lane])
        return acc

    halves = (x_hi, 1 - x_hi)

    def lower_term(n):
        h = halves[n]

        @pl.loop(0, 4)
        def _(b):
            rs = pl.ds(pl.multiple_of(b * BLK, 16), BLK)
            lt[h, rs, :] = -(w_re * xi[h, rs, :] + w_im * xr[h, rs, :])

    def z_at(b):
        return b * BLK

    def y_at(b):
        return z * BLK + b * SUB

    z_ring = (z_at, BLK, 144, (zp, zm, z2, z), (d_zp, d_zm), rz1, rz2)

    def y_send(n):
        h = halves[n]
        return [
            send(lt.at[h, rows_of(y_at((col + d) % 4), SUB), :], ry.at[n, d - 1], at_y((col + d) % 4))
            for d in range(1, 4)
        ]

    def y_sum(n, before):
        for c in before:
            c.wait_recv()
        lt[halves[n], rows_of(y_at(col), SUB), :] += ry[n, 0] + ry[n, 1] + ry[n, 2]

    def ring1(n, ring):
        at, size, first, (p, m, two, own), (dp, dm), r1, r2 = ring
        h = halves[n]
        return (
            send(lt.at[h, rows_of(at(two), first), :], r1.at[n, pl.ds(0, first), :], dp),
            send(
                lt.at[h, rows_of(at(two) + first, size - first), :],
                r1.at[n, pl.ds(first, size - first), :], dm,
            ),
        )

    def ring2(n, ring, before):
        at, size, first, (p, m, two, own), (dp, dm), r1, r2 = ring
        h = halves[n]
        before[0].wait_recv()
        lt[h, rows_of(at(p), first), :] += r1[n, 0:first]
        a = send(lt.at[h, rows_of(at(p), size), :], r2.at[n, 0], dp)
        before[1].wait_recv()
        lt[h, rows_of(at(m) + first, size - first), :] += r1[n, first:size]
        return a, send(lt.at[h, rows_of(at(m), size), :], r2.at[n, 1], dm)

    def ring3(n, ring, before):
        at, size, first, (p, m, two, own), (dp, dm), r1, r2 = ring
        before[0].wait_recv()
        before[1].wait_recv()
        lt[halves[n], rows_of(at(own), size), :] += r2[n, 0] + r2[n, 1]

    def x_swap(n):
        return send(lt.at[halves[n], rows_of(y_at(col), SUB), :], rx.at[n], d_xn)

    def x_add(n, before):
        before.wait_recv()
        ld[halves[n]] = lt[halves[n], rows_of(y_at(col), SUB), :] + rx[n]

    def upper_prep(k):
        lane = lanes(k)
        for q in range(4):
            re, im = uf[q, 0, :, lane], uf[q, 1, :, lane]
            rs = pl.ds(q * Q, Q)
            for part, v in ((0, w_re * re - w_im * im), (1, w_re * im + w_im * re)):
                hi, low = split(v)
                uph[part, rs, lane] = hi
                upl[part, rs, lane] = low

    def upper_chunk(k):
        lane = lanes(k)
        acc = nn(uph[0, :, lane], ah[1, lane, :])
        acc = acc + nn(uph[0, :, lane], al[1, lane, :])
        acc = acc + nn(upl[0, :, lane], ah[1, lane, :])
        acc = acc + nn(uph[1, :, lane], ah[0, lane, :])
        acc = acc + nn(uph[1, :, lane], al[0, lane, :])
        acc = acc + nn(upl[1, :, lane], ah[0, lane, :])
        if k == 0:
            y[...] = acc
        else:
            y[...] += acc

    def chunk(n, k, blocks=(0, 4)):
        dst, h = ((bl, br)[n], halves[n])
        if blocks[0] == 0:
            for q in range(2):
                build(dst, h * 2 + q, q, lanes(k))

        @pl.loop(*blocks)
        def _(b):
            rs = pl.ds(pl.multiple_of(b * BLK, 16), BLK)
            if k == 2:
                acc = nt(ath[rs, :], bt[0]) + nt(ath[rs, :], bt[1]) + nt(atl[rs, :], bt[0])
            else:
                acc = product(rs, lanes(k), dst)
            if k == 0:
                xr[h, rs, :] = acc[:, :128]
                xi[h, rs, :] = acc[:, 128:]
            else:
                xr[h, rs, :] += acc[:, :128]
                xi[h, rs, :] += acc[:, 128:]

    def pivot_chunk(k):
        lane = lanes(k)
        acc = nn(uph[0, :, lane], xih[lane, :])
        acc = acc + nn(uph[0, :, lane], xil[lane, :])
        acc = acc + nn(upl[0, :, lane], xih[lane, :])
        acc = acc + nn(uph[1, :, lane], xrh[lane, :])
        acc = acc + nn(uph[1, :, lane], xrl[lane, :])
        acc = acc + nn(upl[1, :, lane], xrh[lane, :])
        if k == 0:
            pvs[...] = acc
        else:
            pvs[...] += acc

    def choose_rows():
        for b in range(BAT):
            own_s[b] = own_ref[:, b * WIDE : (b + 1) * WIDE]
        mine = own_s[group // 16].astype(F32).astype(BF16)
        here = nn(
            mine,
            (iota((WIDE, NB), 0) == (group % 16) * NB + iota((WIDE, NB), 1)).astype(F32).astype(BF16),
        )
        owner = iota((2 * DEV, NB), 0)
        named = jnp.zeros((2 * DEV, NB), F32)
        for t in range(TOPK):
            hit = here[t : t + 1, :] == (owner // 2).astype(F32)
            named = jnp.maximum(named, hit.astype(F32))
        earlier = (iota((NB, NB), 0) < iota((NB, NB), 1)).astype(F32).astype(BF16)
        rank = nn(named.astype(BF16), earlier)
        chosen = named * (rank == (owner % 2).astype(F32)).astype(F32)
        spot = iota((NB, SUB), 1)
        spread = (
            (spot // 36 == x_lo) & ((spot % 36) // 2 == iota((NB, SUB), 0))
        ).astype(F32)
        wide = nn(chosen.astype(BF16), spread.astype(BF16))
        out = iota((4 * DEV, 2 * DEV), 0)
        repeat = (iota((4 * DEV, 2 * DEV), 1) == out // 2).astype(F32)
        full = nn(repeat.astype(BF16), wide.astype(BF16))
        keep = iota((4 * DEV, SUB), 0) % 2 == iota((4 * DEV, SUB), 1) % 2
        sel[...] = jnp.where(keep, full, 0.0).astype(BF16)

    def choose_ancestors(start, stop):
        if start == 0:
            local_ba.wait()
        block = iota((WIDE, WIDE), 0), iota((WIDE, WIDE), 1)
        earlier = ((block[0] // NB == block[1] // NB) & (block[0] < block[1])).astype(F32)
        earlier = earlier.astype(BF16)
        slot = iota((4 * 16, WIDE), 0)
        wanted = slot - slot % 2

        @pl.loop(start, stop)
        def _(b):
            owners = own_s[b]
            mine = jnp.max((owners == me).astype(F32), 0, keepdims=True)
            rank = nn(jnp.broadcast_to(mine, (8, WIDE)).astype(BF16), earlier)[0:1, :]
            base = (iota((1, WIDE), 1) // NB * 4).astype(F32)
            key = jnp.where(mine > 0, base + 2 * rank, -8.0)
            hit = key == wanted.astype(F32)
            acc = jnp.zeros((4 * 16, 128), F32)
            for parity in range(2):
                one = (hit & (slot % 2 == parity)).astype(F32).astype(BF16)
                v = ba[pl.ds(b * 2 * WIDE + parity, WIDE, stride=2), :]
                hi, low = split(v)
                acc = acc + nn(one, hi) + nn(one, low)
            ba4[rows_of(b * 64, 64), :] = acc

    def exchange(n):
        h = halves[n]
        v = ld[h]
        hi, low = split(v)
        rest = (v - hi.astype(F32) - low.astype(F32)).astype(BF16)
        packed = nn(sel[...], hi) + nn(sel[...], low) + nn(sel[...], rest)
        pk[n] = packed.reshape(DEV, 4, 128)
        got[h, group] = pk[n, me]
        for i in range(1, DEV):
            p, r, c = (pole + i // 16) % 8, (row + i // 4) % 4, (col + i) % 4
            pltpu.make_async_remote_copy(
                src_ref=pk.at[n, (p * 4 + r) * 4 + c], dst_ref=got.at[h, group],
                send_sem=asend.at[n], recv_sem=arecv.at[h],
                device_id=(p, r, c), device_id_type=MESH,
            ).start()

    def three(a, b):
        ahi, alo = split(a)
        bhi, blo = split(b)
        return nn(ahi, bhi) + nn(ahi, blo) + nn(alo, bhi)

    for b in range(1, 4):
        split_a(b)
    local_l.wait()
    l_near[0].wait_recv()
    chunk(0, 0)
    l_near[1].wait_recv()
    chunk(0, 1)
    l_near[2].wait_recv()
    chunk(0, 2)
    ls = [l_share(0, lo[0])]
    lower_term(0)
    zn = ring1(0, z_ring)
    choose_rows()
    uf_moves = [u_forward(0, uo[0])]
    choose_ancestors(0, 4)
    ls[0].wait_recv()
    chunk(1, 0, (0, 2))
    zn = ring2(0, z_ring, zn)
    chunk(1, 0, (2, 4))
    uf_moves.append(u_forward(1, uo[1]))
    ls.append(l_share(1, lo[1]))
    choose_ancestors(4, 8)
    ls.append(l_share(2, lo[2]))
    uf_moves.append(u_forward(2, uo[2]))
    local_u.wait()
    ls[1].wait_recv()
    chunk(1, 1, (0, 2))
    ring3(0, z_ring, zn)
    yn = y_send(0)
    chunk(1, 1, (2, 4))
    ls[2].wait_recv()
    chunk(1, 2)
    lower_term(1)
    zf = ring1(1, z_ring)
    for h in range(2):
        hs = pl.ds(h * 128, 128)
        hi, low = split(xi[h])
        xih[:, hs], xil[:, hs] = hi, low
        hi, low = split(xr[h])
        xrh[:, hs], xrl[:, hs] = hi, low
    for c in uf_moves[0]:
        c.wait_recv()
    upper_prep(0)
    upper_chunk(0)
    y_sum(0, yn)
    xn = x_swap(0)
    pivot_chunk(0)
    zf = ring2(1, z_ring, zf)
    for c in uf_moves[1]:
        c.wait_recv()
    upper_prep(1)
    pivot_chunk(1)
    for c in uf_moves[2]:
        c.wait_recv()
    upper_prep(2)
    pivot_chunk(2)

    place = (iota((Q, S), 1) == iota((Q, S), 0) + col * Q).astype(F32)
    piece = w_re * piv_ref[0, 1] + w_im * piv_ref[0, 0]
    placed = jnp.dot(piece, place, precision=lax.Precision.HIGHEST, preferred_element_type=F32)
    for g in range(32):
        at = (g % 2, (g // 4) % 4, ((g // 2) % 2) * 2 + g // 16)
        mine = (row == g // 8).astype(F32)
        pvb[at[0], at[1], at[2]] = (
            pvs[g * 8 : g * 8 + 8, :] + mine * placed[(g % 8) * 8 : (g % 8) * 8 + 8, :]
        )
    p1 = send(pvb.at[1 - core], pc, d_core)
    x_add(0, xn)
    exchange(0)
    p1.wait_recv()
    pvb[core] += pc[...]

    def in_plane(n):
        zz, xx = (z + n // 4) % 4, (x + n) % 4
        return zz, xx, ((xx % 2) * 4 + zz, (xx // 2) * 2 + core, col)

    p2 = []
    for n in range(1, 16):
        zz, xx, dev = in_plane(n)
        p2.append(send(pvb.at[core, zz, xx], pz.at[n - 1], dev))
    upper_chunk(1)
    ring3(1, z_ring, zf)
    yf = y_send(1)
    upper_chunk(2)
    for g in range(32):
        at = (g % 2, (g // 4) % 4, ((g // 2) % 2) * 2 + g // 16)
        cb[at[0], at[1], at[2]] = -y[g * 8 : g * 8 + 8, :]
    to_core = send(cb.at[1 - core], rc, d_core)
    for c in p2:
        c.wait_recv()
    pb[col] = pvb[core, z, x] + jnp.sum(pz[...], 0)
    p4 = [send(pb.at[col], pb.at[col], at_y((col + d) % 4)) for d in range(1, 4)]
    for g in range(32):
        k = (g % 2) * 16 + ((g // 4) % 4) * 4 + ((g // 2) % 2) * 2 + g // 16
        bsp[k * 8 : k * 8 + 8, :] = bs_ref[g * 8 : g * 8 + 8, :]
    to_core.wait_recv()

    @pl.loop(0, 4)
    def _(b):
        cb[core, b] += rc[b]

    y_sum(1, yf)
    xf = x_swap(1)

    wide, rest = pl.ds(0, LEFT), pl.ds(LEFT, T - LEFT)
    fa = [
        send(cb.at[core, (z + d) % 4, :, :, wide], ra.at[d - 1], at_z((z + d) % 4))
        for d in range(1, 4)
    ]
    fb = [
        send(cb.at[core, :, (x + d) % 4, :, rest], rb.at[d - 1], at_x((x + d) % 4))
        for d in range(1, 4)
    ]
    for c in p4:
        c.wait_recv()
    pfull[core, z, x] = pb[0] + pb[1] + pb[2] + pb[3]
    p5 = []
    for n in range(1, 16):
        zz, xx, dev = in_plane(n)
        p5.append(send(pfull.at[core, z, x], pfull.at[core, z, x], dev))
    x_add(1, xf)
    exchange(1)
    for c in fb:
        c.wait_recv()
    cb[core, :, x, :, LEFT:] += rb[0] + rb[1] + rb[2]
    hb = [
        send(cb.at[core, (z + d) % 4, x, :, rest], rv.at[d - 1, :, rest], at_z((z + d) % 4))
        for d in range(1, 4)
    ]
    for c in fa:
        c.wait_recv()
    cb[core, z, :, :, :LEFT] += ra[0] + ra[1] + ra[2]
    ha = [
        send(cb.at[core, z, (x + d) % 4, :, wide], rv.at[d - 1, :, wide], at_x((x + d) % 4))
        for d in range(1, 4)
    ]
    for c in p5:
        c.wait_recv()
    p6 = send(pfull.at[core], pfull.at[core], d_core)
    for c in hb + ha:
        c.wait_recv()
    out_ref[:, :T] = cb[core, z, x] + rv[0] + rv[1] + rv[2]
    p6.wait_recv()
    pivot = pfull[...].reshape(S, S)
    charge = jnp.sum(bsp[...] * three(pivot, bs_ref[...]), 0, keepdims=True)
    others = pl.ds(0, DEV - 1)
    for h in range(2):
        pltpu.make_async_copy(got.at[h, others], got.at[h, others], arecv.at[h]).wait()
    received = jnp.concatenate([got[h].reshape(4 * DEV, 128) for h in range(2)], 1)
    projected = three(received, bs_ref[...])
    charge = charge + jnp.sum(ba4[...] * projected, 0, keepdims=True)
    out_ref[:, T:] = jnp.broadcast_to(charge, (8, 128))
    for n in range(2):
        pltpu.make_async_copy(pk.at[n, others], pk.at[n, others], asend.at[n]).wait()
    for c in started:
        c.wait_send()


N_COPIES = 112


def hand_out(both_ref, upper_ref, charge_ref):
    upper_ref[...] = both_ref[:, :T]
    charge_ref[...] = both_ref[0:1, T:]


def fused(weights, tile, lower, upper, pivot, owners, basis_super, basis_ancestor):
    vmem = pl.BlockSpec(memory_space=pltpu.VMEM)
    hbm = pl.BlockSpec(memory_space=pl.ANY)
    return pl.pallas_call(
        kernel,
        out_shape=jax.ShapeDtypeStruct((8, T + 128), F32),
        in_specs=[pl.BlockSpec(memory_space=pltpu.SMEM), hbm, hbm, hbm, vmem, vmem, vmem, hbm],
        out_specs=vmem,
        scratch_shapes=[
            pltpu.VMEM((2, T, T), F32),
            pltpu.VMEM((2, T, T), BF16),
            pltpu.VMEM((2, T, T), BF16),
            pltpu.VMEM((4, 2, Q, T), F32),
            pltpu.VMEM((4, 2, Q, T), F32),
            pltpu.VMEM((4, S, T), BF16),
            pltpu.VMEM((4, S, T), BF16),
            pltpu.VMEM((2, S, T), BF16),
            pltpu.VMEM((2, S, T), BF16),
            pltpu.VMEM((2, T, 128), F32),
            pltpu.VMEM((2, T, 128), F32),
            pltpu.VMEM((T, S), BF16),
            pltpu.VMEM((T, S), BF16),
            pltpu.VMEM((T, S), BF16),
            pltpu.VMEM((T, S), BF16),
            pltpu.VMEM((S, T), F32),
            pltpu.VMEM((2, T, 128), F32),
            pltpu.VMEM((2, BLK, 128), F32),
            pltpu.VMEM((2, 2, BLK, 128), F32),
            pltpu.VMEM((2, 3, SUB, 128), F32),
            pltpu.VMEM((2, SUB, 128), F32),
            pltpu.VMEM((2, SUB, 128), F32),
            pltpu.VMEM((2, 4, 4, 8, T), F32),
            pltpu.VMEM((4, 4, 8, T), F32),
            pltpu.VMEM((3, 4, 8, LEFT), F32),
            pltpu.VMEM((3, 4, 8, T - LEFT), F32),
            pltpu.VMEM((3, 8, T), F32),
            pltpu.VMEM((2, 4, 4, 8, S), F32),
            pltpu.VMEM((4, 4, 8, S), F32),
            pltpu.VMEM((15, 8, S), F32),
            pltpu.VMEM((4, 8, S), F32),
            pltpu.VMEM((2, 4, 4, 8, S), F32),
            pltpu.VMEM((S, 128), F32),
            pltpu.VMEM((4608, 128), F32),
            pltpu.VMEM((4 * DEV, 128), F32),
            pltpu.VMEM((4 * DEV, SUB), BF16),
            pltpu.VMEM((2, DEV, 4, 128), F32),
            pltpu.VMEM((2, DEV, 4, 128), F32),
            pltpu.VMEM((BAT, TOPK, WIDE), jnp.int32),
            pltpu.VMEM((S, S), F32),
            pltpu.VMEM((T, S), BF16),
            pltpu.VMEM((T, S), BF16),
            pltpu.VMEM((2, S, S), BF16),
            pltpu.SemaphoreType.DMA((N_COPIES,)),
            pltpu.SemaphoreType.DMA((N_COPIES,)),
            pltpu.SemaphoreType.DMA((7,)),
            pltpu.SemaphoreType.DMA((2,)),
            pltpu.SemaphoreType.DMA((2,)),
        ],
        compiler_params=pltpu.CompilerParams(
            collective_id=0, has_side_effects=True, vmem_limit_bytes=63 << 20
        ),
    )(weights, tile, lower, upper, pivot, owners, basis_super, basis_ancestor)


def body(
    inverse_tile, lower_factor, upper_factor, pivot_inverse, pole_weights, block_owners,
    basis_ancestor, basis_super,
):
    out = fused(
        pole_weights, inverse_tile, lower_factor, upper_factor, pivot_inverse, block_owners.T,
        basis_super, basis_ancestor,
    )
    upper_density, charge = pl.pallas_call(
        hand_out,
        out_shape=(jax.ShapeDtypeStruct((8, T), F32), jax.ShapeDtypeStruct((1, 128), F32)),
    )(out)
    return (upper_density, charge.reshape(128))


def solution(mesh):
    placed = (
        P("pole", None, "row", "col"),
        P("pole", None, "row", "col"),
        P("pole", None, "col", "row"),
        P("pole", None, "row", "col"),
        P("pole", None),
        P(),
        P(None, ("pole", "row", "col")),
        P(None, ("pole", "row", "col")),
    )
    return jax.shard_map(
        body,
        mesh=mesh,
        in_specs=placed,
        out_specs=(P(("pole", "row"), "col"), P(("pole", "row", "col"))),
        check_vma=False,
    )
```
